32 devices in a mesh: groups: 2 (over x), ctx: 16 (over z, y, core).
Axes of the slice: x: 2, y: 2, z: 4, core: 2. Of those that a mesh axis runs over, the one named last changes fastest.
Arguments:
- query: bfloat16 [8192, 1024], P(('groups', 'ctx')), parts along dimension 0, may hold values from -130 to 130, as said below
- key: bfloat16 [8192, 1024], P(('groups', 'ctx')), parts along dimension 0, may hold values from -4.5 to 4.5
- value: bfloat16 [8192, 1024], P(('groups', 'ctx')), parts along dimension 0, may hold values from -6 to 6
- cotangent: bfloat16 [8192, 1024], P(('groups', 'ctx')), parts along dimension 0, may hold values from -6 to 6
- global_ids: int32 [4], P('groups'), parts along dimension 0, may hold values from 0 to 63
- rand_owner: int32 [128, 6], P('groups'), parts along dimension 0, may hold values from 0 to 15, all different within a row; in each aligned block of 4 rows (0 to 3, 4 to 7, ...) at most 2 rows name the same one
- rand_local: int32 [128, 6], P('groups'), parts along dimension 0, may hold values from 0 to 3
Outputs:
- attended: bfloat16 [8192, 1024], P(('groups', 'ctx')), parts along dimension 0
- grad_query: bfloat16 [8192, 1024], P(('groups', 'ctx')), parts along dimension 0
- grad_key: bfloat16 [8192, 1024], P(('groups', 'ctx')), parts along dimension 0
- grad_value: bfloat16 [8192, 1024], P(('groups', 'ctx')), parts along dimension 0
The draws below stay inside these ranges and needn't reach their ends.
There are 2 independent parts, one for each index of `groups`. The reference program is written for one: setup_inputs(seed, part) draws one part's arguments, and reference() takes and returns one part's arrays. A program takes and returns all parts, laid end to end along the dimension named above; each array names one. Nothing has to cross between parts.
Inputs may be any that keep to these rules, and one draw needn't show every extreme that they name: query and key are drawn together. `rand_owner`: each row names 6 different devices. In the 4 rows of one device no device is named more than 2 times, and in some device's rows some device is named exactly 2 times.
All inputs are finite; a program needn't handle non-finite values.
Results may differ from the reference program's by a relative error of at most 0.017.
Values may be sent and summed in bfloat16 or wider, within the bound.
A program may use at most 192 MiB of HBM per device.

```python
import math
import jax
import jax.numpy as jnp
import numpy as np
from jax import lax

HEAD_DIM = 64
HEADS = 16
GROUP_HEADS = 8
BLOCK = 64
GLOBALS = 2
ROUNDS = 3
BLK_DEV = 4
FEAT = 1024
HG = 2
NB = 64
TOKENS = 4096
SLOT = 2
N_CTX = 16


def paired_draw(base_key):
    mixed = jax.random.fold_in(base_key, 4021)
    first, second = jax.random.split(mixed, 2)
    shape = (TOKENS, HEADS * HEAD_DIM)
    key_part = jnp.clip(jax.random.normal(first, shape, jnp.float32), -4.0, 4.0)
    query_part = jnp.clip(jax.random.normal(second, shape, jnp.float32), -4.0, 4.0)
    return (query_part, key_part)


def draw_query(key, part):
    return paired_draw(key)[0].astype(jnp.bfloat16)


def draw_key(key, part):
    return paired_draw(key)[1].astype(jnp.bfloat16)


def set_ends(array, own_key, least, high):
    longest = array.shape.index(max(array.shape))
    spots = []
    for shift in (0, 1):
        where = [jax.random.randint(jax.random.fold_in(own_key, axis), (), 0, length) for axis, length in enumerate(array.shape)]
        where[longest] = (where[longest] + shift) % array.shape[longest]
        spots.append(tuple(where))
    return array.at[spots[0]].set(least).at[spots[1]].set(high)


def steps_of(stream_key, dims, pieces, low, top_value):
    def one(dim, shards_of):
        steps = jax.random.uniform(jax.random.fold_in(jax.random.fold_in(stream_key, 6), dim), (shards_of,), jnp.float32, low / len(pieces), top_value / len(pieces))
        return jnp.repeat(jnp.exp(steps), dims[dim] // shards_of).reshape((-1,) + (1,) * (len(dims) - dim - 1))

    level = one(*pieces[0])
    for cut in pieces[1:]:
        level = level * one(*cut)
    return level


def shared_out(own_key, own, number, rows, count, top, reach, skew):
    ranking = jax.random.permutation(own_key, count)
    heavy_load, ordinary = portions_of(count, rows * top, reach, skew, True), portions_of(count, rows * top, reach, skew, False)
    places = jnp.arange(count)

    def named(sizes, rotation):
        used = int((sizes > 0).sum())
        fixed = max(1, used // 4)
        moved = fixed + (places - fixed + rotation * (used - fixed)) % max(1, count - fixed)
        return jnp.zeros((count,), jnp.int32).at[ranking[jnp.where(places < fixed, places, moved)]].set(jnp.asarray(sizes, jnp.int32))

    sizes = jnp.where(number % 4 == 0, named(heavy_load, number // 4), named(ordinary, number - number // 4 - 1))
    mixed = jax.random.permutation(jax.random.fold_in(own, 3), count)
    giver, sink = mixed[0:count // 2 * 2:2], mixed[1:count // 2 * 2:2]
    slack = jnp.minimum(sizes[giver] - 1, reach - sizes[sink]) // 2
    slack = jnp.where((giver == ranking[0]) | (sink == ranking[0]) | (sizes[sink] == 0), 0, jnp.maximum(slack, 0))
    moved = jax.random.randint(jax.random.fold_in(own, 4), (count // 2,), 0, 1 << 20) % (slack + 1)
    sizes = sizes.at[giver].add(-moved).at[sink].add(moved)
    items = jnp.searchsorted(jnp.cumsum(sizes), jnp.arange(rows * top), side="right").astype(jnp.int32)
    listing = items.reshape(top, rows).T
    listing = listing[jax.random.permutation(jax.random.fold_in(own, 1), rows)]
    rotation = jax.random.randint(jax.random.fold_in(own, 2), (rows, 1), 0, top)
    return jnp.take_along_axis(listing, (jnp.arange(top)[None, :] + rotation) % top, axis=1)


def portions_of(count, total, most, skew, full):
    portions = [(1 << 20) // math.isqrt(rank ** skew) + 1 for rank in range(1, count + 1)]
    largest = most if full else min(most, max(-(-total // count), total * portions[0] // sum(portions)))
    least = 1 if total - largest >= count - 1 else 0
    holding, rest = [largest] + [least] * (count - 1), total - largest - least * (count - 1)
    while rest > 0:
        candidates = [i for i in range(1, count) if holding[i] < largest] or [i for i in range(1, count) if holding[i] < most]
        pool, remaining = sum([portions[i] for i in candidates]), rest
        for i in candidates:
            extra = min(most - holding[i], max(1, remaining * portions[i] // pool), rest)
            holding[i] = holding[i] + extra
            rest = rest - extra
    return np.array(holding)


def bell_draw(rng, shape, width, bound, pieces=(), held_as=jnp.bfloat16):
    factor_of = steps_of(rng, shape, pieces, -0.22, 0.18) if pieces else 1.0
    values = jax.random.normal(rng, shape, jnp.float32) * width * factor_of
    return jnp.minimum(jnp.maximum(values, -bound), bound).astype(held_as)


def setup_inputs(seed: int = 0, part: int = 0) -> dict:
    arg_keys = jax.random.split(jax.random.key(seed), 8)
    own_keys = jax.random.split(jax.random.fold_in(arg_keys[7], part), 8)
    query = draw_query(jax.random.fold_in(jax.random.fold_in(arg_keys[7], part), 71), part)
    key = draw_key(jax.random.fold_in(jax.random.fold_in(arg_keys[7], part), 71), part)
    value = bell_draw(own_keys[2], (TOKENS, FEAT), 1.0, 6.0, ((0, 16),))
    cotangent = bell_draw(own_keys[3], (TOKENS, FEAT), 1.0, 6.0, ((0, 16),))
    global_ids = jax.random.randint(own_keys[4], (GLOBALS,), 0, NB).astype(jnp.int32)
    rand_owner_keys = jax.random.split(jax.random.fold_in(own_keys[5], 1), NB // BLK_DEV)
    rand_owner_turns = jax.random.permutation(jax.random.fold_in(own_keys[5], 3), NB // BLK_DEV)
    rand_owner = jax.vmap(lambda own, number: shared_out(jax.random.fold_in(own_keys[5], 2), own, number, BLK_DEV, N_CTX, HG * ROUNDS, SLOT, 2))(rand_owner_keys, rand_owner_turns).reshape((NB, HG * ROUNDS))
    rand_local = set_ends(jax.random.randint(own_keys[6], (NB, HG * ROUNDS), 0, BLK_DEV), jax.random.fold_in(own_keys[6], 1), 0, BLK_DEV - 1).astype(jnp.int32)
    return dict(query=query, key=key, value=value, cotangent=cotangent, global_ids=global_ids, rand_owner=rand_owner, rand_local=rand_local)


NEG_FILL = -1.0e30


def reference(query, key, value, cotangent, global_ids, rand_owner, rand_local):
    features = HEADS * HEAD_DIM
    groups = HEADS // GROUP_HEADS
    key_kinds = 3 + GLOBALS + ROUNDS
    key_span = key_kinds * BLOCK
    score_scale = HEAD_DIM ** -0.5
    query_five = query.reshape(NB, BLOCK, groups, GROUP_HEADS, HEAD_DIM)
    key_five = key.reshape(NB, BLOCK, groups, GROUP_HEADS, HEAD_DIM)
    value_five = value.reshape(NB, BLOCK, groups, GROUP_HEADS, HEAD_DIM)
    cot_five = cotangent.reshape(NB, BLOCK, groups, GROUP_HEADS, HEAD_DIM)
    rand_ids = (rand_owner * BLK_DEV + rand_local).astype(jnp.int32).reshape(NB, groups, ROUNDS)
    glob_ids = global_ids.astype(jnp.int32)
    group_col = jnp.arange(groups, dtype=jnp.int32)[:, None]

    def one_block(grad_pair, block_index):
        grad_k, grad_v = grad_pair
        window_raw = block_index + jnp.arange(-1, 2, dtype=jnp.int32)
        window_ok = (window_raw >= 0) & (window_raw < NB)
        window_ids = jnp.clip(window_raw, 0, NB - 1).astype(jnp.int32)
        picked = rand_ids[block_index]

        def collect(table):
            win_part = jnp.transpose(table[window_ids], (2, 3, 0, 1, 4))
            glob_part = jnp.transpose(table[glob_ids], (2, 3, 0, 1, 4))
            rand_part = jnp.transpose(table[picked, :, group_col], (0, 3, 1, 2, 4))
            joined = jnp.concatenate((win_part, glob_part, rand_part), axis=2)
            return joined.reshape(groups, GROUP_HEADS, key_span, HEAD_DIM).astype(jnp.float32)

        keys_all = collect(key_five)
        vals_all = collect(value_five)
        key_valid = jnp.concatenate((jnp.repeat(window_ok, BLOCK), jnp.ones(((GLOBALS + ROUNDS) * BLOCK,), jnp.bool_)))
        q_block = query_five[block_index].astype(jnp.float32)
        d_block = cot_five[block_index].astype(jnp.float32)
        scores = jnp.einsum('qghd,ghkd->ghqk', q_block, keys_all) * score_scale
        scores = jnp.where(key_valid, scores, NEG_FILL)
        row_max = jnp.max(scores, axis=-1, keepdims=True)
        weights = jnp.where(key_valid, jnp.exp(scores - row_max), 0.0)
        log_total = row_max + jnp.log(jnp.sum(weights, axis=-1, keepdims=True))
        probs = jnp.where(key_valid, jnp.exp(scores - log_total), 0.0)
        probs_b = probs.astype(jnp.bfloat16).astype(jnp.float32)
        attended = jnp.einsum('ghqk,ghkd->qghd', probs_b, vals_all).astype(jnp.bfloat16)
        row_dot = jnp.sum(d_block * attended.astype(jnp.float32), axis=-1)
        row_dot = jnp.transpose(row_dot, (1, 2, 0))[..., None]
        dprob = jnp.einsum('qghd,ghkd->ghqk', d_block, vals_all)
        dscore = (probs * (dprob - row_dot)).astype(jnp.bfloat16).astype(jnp.float32)
        grad_q = (jnp.einsum('ghqk,ghkd->qghd', dscore, keys_all) * score_scale).astype(jnp.bfloat16)
        term_k = jnp.einsum('ghqk,qghd->ghkd', dscore, q_block) * score_scale
        term_v = jnp.einsum('ghqk,qghd->ghkd', probs_b, d_block)

        def spread(total, term):
            term = term.reshape(groups, GROUP_HEADS, key_kinds, BLOCK, HEAD_DIM)
            win_term = jnp.transpose(term[:, :, 0:3], (2, 3, 0, 1, 4))
            glob_term = jnp.transpose(term[:, :, 3:3 + GLOBALS], (2, 3, 0, 1, 4))
            rand_term = jnp.transpose(term[:, :, 3 + GLOBALS:], (0, 2, 3, 1, 4))
            rand_term = lax.optimization_barrier(rand_term.astype(jnp.bfloat16)).astype(jnp.float32)
            total = total.at[window_ids].add(win_term)
            total = total.at[glob_ids].add(glob_term)
            total = total.at[picked, :, group_col].add(rand_term)
            return total

        return (spread(grad_k, term_k), spread(grad_v, term_v)), (attended, grad_q)

    zero_grad = jnp.zeros((NB, BLOCK, groups, GROUP_HEADS, HEAD_DIM), jnp.float32)
    grads, stacked = lax.scan(one_block, (zero_grad, zero_grad), jnp.arange(NB, dtype=jnp.int32))
    attended = stacked[0].reshape(NB * BLOCK, features)
    grad_query = stacked[1].reshape(NB * BLOCK, features)
    grad_key = grads[0].reshape(NB * BLOCK, features).astype(jnp.bfloat16)
    grad_value = grads[1].reshape(NB * BLOCK, features).astype(jnp.bfloat16)
    return attended, grad_query, grad_key, grad_value
```

```python
import functools

import jax
import jax.numpy as jnp
from jax import lax
from jax.experimental import pallas as pl
from jax.experimental.pallas import tpu as pltpu
from jax.sharding import PartitionSpec as P

HEAD_DIM = 64
GROUP_HEADS = 8
BLOCK = 64
GLOBALS = 2
ROUNDS = 3
PAIR = 2 * HEAD_DIM
NEG_FILL = -1e30
SCALE = HEAD_DIM ** (-0.5)
MESH = pl.DeviceIdType.MESH


def lanes_joined(left, right):
    return jnp.concatenate([left, right], axis=1)


def fused_kernel(
    count,
    shares,
    glob_hbm,
    owner_hbm,
    local_hbm,
    q_hbm,
    k_hbm,
    v_hbm,
    d_hbm,
    att_ref,
    gq_ref,
    gk_ref,
    gv_ref,
    kv_pack,
    qd_pack,
    kv_all,
    qd_all,
    qo_put,
    qo_got,
    gkv_put,
    gkv_got,
    acc_ref,
    chain_ref,
    glob_ref,
    q_ref,
    k_ref,
    v_ref,
    d_ref,
    owner_vec,
    local_vec,
    table_vec,
    glob_ids,
    owner_ref,
    local_ref,
    table,
    fetch,
    drain,
    kv_out,
    kv_in,
    qd_out,
    qd_in,
    qo_out,
    qo_in,
    gkv_out,
    gkv_in,
):
    me = lax.axis_index("ctx")
    heads, tokens = kv_pack.shape[:2]
    blocks = tokens // BLOCK
    own_tokens = tokens // shares
    own_blocks = own_tokens // BLOCK
    all_blocks = count * blocks
    entries = count * own_blocks * ROUNDS
    my_share = lax.rem(me, shares)
    my_head = me // shares
    my_group = my_head // GROUP_HEADS
    my_rows = pl.ds(pl.multiple_of(my_share * own_tokens, own_tokens), own_tokens)

    pulls = [
        pltpu.make_async_copy(source, target, fetch.at[index])
        for index, (source, target) in enumerate(
            (
                (k_hbm, k_ref),
                (v_hbm, v_ref),
                (q_hbm, q_ref),
                (d_hbm, d_ref),
                (owner_hbm, owner_ref),
                (local_hbm, local_ref),
                (owner_hbm, owner_vec),
                (local_hbm, local_vec),
                (glob_hbm, glob_ids),
            )
        )
    ]
    for pull in pulls:
        pull.start()
    barrier = pltpu.get_barrier_semaphore()
    for step in range(1, count):
        peer = lax.rem(me + step, count)
        pl.semaphore_signal(barrier, inc=1, device_id={"ctx": peer}, device_id_type=MESH)

    def pack(left_ref, right_ref, out_ref):
        for pair in range(heads // 2):
            cols = slice(pair * PAIR, (pair + 1) * PAIR)
            left = left_ref[:, cols]
            right = right_ref[:, cols]
            out_ref[2 * pair] = lanes_joined(left[:, :HEAD_DIM], right[:, :HEAD_DIM])
            out_ref[2 * pair + 1] = lanes_joined(left[:, HEAD_DIM:], right[:, HEAD_DIM:])

    pulls[0].wait()
    pulls[1].wait()
    pack(k_ref, v_ref, kv_pack)
    pulls[2].wait()
    pulls[3].wait()
    pack(q_ref, d_ref, qd_pack)
    pl.semaphore_wait(barrier, count - 1)

    def kv_copy(dest, came):
        return pltpu.make_async_remote_copy(
            src_ref=kv_pack.at[dest // shares].reshape(blocks, BLOCK, PAIR),
            dst_ref=kv_all.at[pl.ds(came * blocks, blocks)],
            send_sem=kv_out.at[dest],
            recv_sem=kv_in.at[came],
            device_id={"ctx": dest},
            device_id_type=MESH,
        )

    def qd_copy(dest, came):
        start = pl.multiple_of(lax.rem(dest, shares) * own_tokens, own_tokens)
        return pltpu.make_async_remote_copy(
            src_ref=qd_pack.at[dest // shares, pl.ds(start, own_tokens)],
            dst_ref=qd_all.at[came],
            send_sem=qd_out.at[dest],
            recv_sem=qd_in.at[came],
            device_id={"ctx": dest},
            device_id_type=MESH,
        )

    def row_copy(put_ref, got_ref, out_sem, in_sem):
        def copy(dest, came):
            return pltpu.make_async_remote_copy(
                src_ref=put_ref.at[dest],
                dst_ref=got_ref.at[came],
                send_sem=out_sem.at[dest],
                recv_sem=in_sem.at[came],
                device_id={"ctx": dest},
                device_id_type=MESH,
            )

        return copy

    qo_copy = row_copy(qo_put, qo_got, qo_out, qo_in)
    gkv_copy = row_copy(gkv_put, gkv_got, gkv_out, gkv_in)

    for step in range(1, count):
        kv_copy(lax.rem(me + count - step, count), me).start()
    for step in range(1, count):
        qd_copy(lax.rem(me + count - step, count), me).start()

    for part in range(blocks):
        kv_all[me * blocks + part] = kv_pack[my_head, part * BLOCK : (part + 1) * BLOCK]
    qd_all[me] = qd_pack[my_head, my_rows, :]
    acc_ref[...] = jnp.zeros_like(acc_ref)
    glob_ref[...] = jnp.zeros_like(glob_ref)
    chain_ref[entries] = jnp.zeros_like(chain_ref[entries])

    for pull in pulls[4:]:
        pull.wait()
    first_row = my_group * ROUNDS
    rows = pl.ds(first_row, ROUNDS)
    places = owner_vec[rows, :] * blocks + local_vec[rows, :]
    block_of = lax.broadcasted_iota(jnp.int32, (ROUNDS, all_blocks), 1)
    round_of = lax.broadcasted_iota(jnp.int32, (ROUNDS, all_blocks), 0)
    turn = lax.rem(lax.div(block_of, blocks) + (count - me), count)
    part_of = lax.rem(block_of, blocks) - my_share * own_blocks
    order = (turn * own_blocks + part_of) * ROUNDS + round_of
    order = jnp.where((part_of >= 0) & (part_of < own_blocks), order, -1)
    lane_block = lax.broadcasted_iota(jnp.int32, (1, all_blocks), 1)

    def link(step, carry):
        before, last = carry
        peer = lax.rem(me + step, count)
        for part in range(own_blocks):
            block = peer * blocks + my_share * own_blocks + part
            for kind in range(ROUNDS):
                entry = (step * own_blocks + part) * ROUNDS + kind
                place = (
                    owner_ref[first_row + kind, block] * blocks + local_ref[first_row + kind, block]
                )
                before = jnp.where((places == place) & (order > entry), entry, before)
                last = jnp.where(lane_block == place, entry, last)
        return before, last

    before, last = lax.fori_loop(
        0,
        count,
        link,
        (
            jnp.full((ROUNDS, all_blocks), entries, jnp.int32),
            jnp.full((1, all_blocks), entries, jnp.int32),
        ),
    )
    which = jnp.zeros((1, all_blocks), jnp.int32)
    for index in range(GLOBALS):
        which += jnp.where(lane_block == glob_ids[index], 1 << index, 0)
    table_vec[0:ROUNDS, :] = places
    table_vec[ROUNDS : 2 * ROUNDS, :] = before
    table_vec[2 * ROUNDS : 2 * ROUNDS + 1, :] = last
    table_vec[2 * ROUNDS + 1 : 2 * ROUNDS + 2, :] = which
    to_scalar = pltpu.make_async_copy(table_vec, table, fetch.at[len(pulls)])
    to_scalar.start()
    to_scalar.wait()

    for step in range(1, count):
        peer = lax.rem(me + step, count)
        kv_copy(peer, peer).wait_recv()

    lane = lax.broadcasted_iota(jnp.int32, (BLOCK, PAIR), 1)
    low = lane < HEAD_DIM
    row_lane = lax.broadcasted_iota(jnp.int32, (1, PAIR), 1)
    contract_last = (((1,), (1,)), ((), ()))
    contract_first = (((0,), (0,)), ((), ()))

    def load(peer, part):
        block = peer * blocks + my_share * own_blocks + part
        qd = qd_all[peer, part * BLOCK : (part + 1) * BLOCK, :]
        near = [lax.rem(block + all_blocks - 1, all_blocks), lax.rem(block + 1, all_blocks), block]
        spots = near + [glob_ids[kind] for kind in range(GLOBALS)]
        spots = spots + [table[kind, block] for kind in range(ROUNDS)]
        kv = jnp.concatenate([kv_all[p] for p in spots], axis=0)
        zero = jnp.zeros_like(qd)
        diag = jnp.concatenate(
            [jnp.where(low, qd * jnp.bfloat16(SCALE), zero), jnp.where(low, zero, qd)], axis=0
        )
        both = lax.dot_general(diag, kv, contract_last, preferred_element_type=jnp.float32)
        return block, near, qd, kv, diag, both

    def soften(block, both):
        scores = both[:BLOCK]
        bias = jnp.where(
            row_lane < BLOCK,
            jnp.where(block == 0, NEG_FILL, 0.0),
            jnp.where(block == all_blocks - 1, NEG_FILL, 0.0),
        ).astype(jnp.float32)
        scores = lanes_joined(scores[:, :PAIR] + bias, scores[:, PAIR:])
        row_max = jnp.max(scores, axis=1, keepdims=True)
        weights = jnp.exp(scores - row_max)
        probs = weights * (1.0 / jnp.sum(weights, axis=1, keepdims=True))
        return probs, probs.astype(jnp.bfloat16)

    def finish(peer, step, part, block, qd, kv, diag, both, probs, probs_b, attended):
        row_dot = jnp.sum(
            jnp.where(low, 0.0, qd.astype(jnp.float32) * attended.astype(jnp.float32)),
            axis=1,
            keepdims=True,
        )
        dscore = (probs * (both[BLOCK:] - row_dot)).astype(jnp.bfloat16)
        grad_q = jnp.dot(dscore, kv, preferred_element_type=jnp.float32) * SCALE
        qo_put[peer, part * BLOCK : (part + 1) * BLOCK, :] = jnp.where(
            low, grad_q.astype(jnp.bfloat16), attended
        )
        terms = lax.dot_general(
            jnp.concatenate([dscore, probs_b], axis=0),
            diag,
            contract_first,
            preferred_element_type=jnp.float32,
        )
        return terms

    def front(peer, step):
        stage = [load(peer, part) for part in range(own_blocks)]
        soft = [soften(block, both) for block, _, _, _, _, both in stage]
        seen = [
            jnp.dot(probs_b, kept[3], preferred_element_type=jnp.float32).astype(jnp.bfloat16)
            for kept, (_, probs_b) in zip(stage, soft)
        ]
        return [
            (
                block,
                near,
                finish(peer, step, part, block, qd, kv, diag, both, *soft[part], seen[part]),
            )
            for part, (block, near, qd, kv, diag, both) in enumerate(stage)
        ]

    def step_of(step, carry):
        peer = lax.rem(me + step, count)

        @pl.when(step > 0)
        def _():
            qd_copy(peer, peer).wait_recv()

        done = front(peer, step)
        for part, (block, near, terms) in enumerate(done):
            for kind in range(3):
                spot = pl.ds(pl.multiple_of(near[kind] * BLOCK, BLOCK), BLOCK)
                acc_ref[spot, :] += terms[kind * BLOCK : (kind + 1) * BLOCK]
            for kind in range(ROUNDS):
                start = (3 + GLOBALS + kind) * BLOCK
                term = terms[start : start + BLOCK].astype(jnp.bfloat16).astype(jnp.float32)
                entry = (step * own_blocks + part) * ROUNDS + kind
                chain_ref[entry] = chain_ref[table[ROUNDS + kind, block]] + term
        shared = functools.reduce(
            jnp.add, [terms[3 * BLOCK : (3 + GLOBALS) * BLOCK] for _, _, terms in done]
        )
        for index in range(GLOBALS):
            own = shared[index * BLOCK : (index + 1) * BLOCK]
            for mix in range(1, 1 << GLOBALS):
                if mix >> index & 1:
                    glob_ref[mix] += own

        @pl.when(step > 1)
        def _():
            qo_copy(lax.rem(me + step - 1, count), me).start()

        return carry

    lax.fori_loop(0, count, step_of, 0)
    qo_copy(lax.rem(me + count - 1, count), me).start()

    def total_of(step, carry):
        dest = lax.rem(me + count - step, count)
        for part in range(blocks):
            block = dest * blocks + part
            spot = pl.ds(pl.multiple_of(block * BLOCK, BLOCK), BLOCK)
            total = acc_ref[spot, :] + chain_ref[table[2 * ROUNDS, block]]
            total = total + glob_ref[table[2 * ROUNDS + 1, block]]
            gkv_put[dest, part * BLOCK : (part + 1) * BLOCK, :] = total.astype(jnp.bfloat16)

        @pl.when(step > 0)
        def _():
            gkv_copy(dest, me).start()

        return carry

    lax.fori_loop(0, count, total_of, 0)
    qo_got[me] = qo_put[me]
    gkv_got[me] = gkv_put[me]

    for step in range(1, count):
        peer = lax.rem(me + step, count)
        qo_copy(peer, peer).wait_recv()
    for pair in range(heads // 2):
        cols = slice(pair * PAIR, (pair + 1) * PAIR)
        for share in range(shares):
            part = slice(share * own_tokens, (share + 1) * own_tokens)
            even = qo_got[2 * pair * shares + share]
            odd = qo_got[(2 * pair + 1) * shares + share]
            q_ref[part, cols] = lanes_joined(even[:, :HEAD_DIM], odd[:, :HEAD_DIM])
            d_ref[part, cols] = lanes_joined(even[:, HEAD_DIM:], odd[:, HEAD_DIM:])
    pushes = [
        pltpu.make_async_copy(source, target, fetch.at[place])
        for place, (source, target) in enumerate(((q_ref, gq_ref), (d_ref, att_ref)))
    ]
    for push in pushes:
        push.start()
    for step in range(1, count):
        peer = lax.rem(me + step, count)
        kv_copy(peer, me).wait_send()
        qd_copy(peer, me).wait_send()
        qo_copy(peer, me).wait_send()

    def head_of(head):
        for share in range(shares):
            source = head * shares + share

            @pl.when(source != me)
            def _():
                gkv_copy(source, source).wait_recv()

        total = gkv_got[head * shares]
        if shares > 1:
            total = total.astype(jnp.float32)
            for share in range(1, shares):
                total += gkv_got[head * shares + share].astype(jnp.float32)
            total = total.astype(jnp.bfloat16)
        return total

    for pair in range(heads // 2):
        cols = slice(pair * PAIR, (pair + 1) * PAIR)
        even = head_of(2 * pair)
        odd = head_of(2 * pair + 1)
        k_ref[:, cols] = lanes_joined(even[:, :HEAD_DIM], odd[:, :HEAD_DIM])
        v_ref[:, cols] = lanes_joined(even[:, HEAD_DIM:], odd[:, HEAD_DIM:])
        for place, (source, target) in enumerate(((k_ref, gk_ref), (v_ref, gv_ref))):
            push = pltpu.make_async_copy(
                source.at[:, cols], target.at[:, cols], drain.at[place, pair]
            )
            push.start()
            pushes.append(push)
    for step in range(1, count):
        gkv_copy(lax.rem(me + step, count), me).wait_send()
    for push in pushes:
        push.wait()


def store_kernel(*refs):
    size = (len(refs) - 3) // 2
    hold, come, go = refs[2 * size :]
    half = hold.shape[1] // 2
    pulls, pushes = [], []
    for index in range(size):
        for part in range(2):
            rows = pl.ds(part * half, half)
            here = hold.at[index, rows]
            pulls.append(pltpu.make_async_copy(refs[index].at[rows], here, come.at[index, part]))
            pushes.append(
                pltpu.make_async_copy(here, refs[size + index].at[rows], go.at[index, part])
            )
    for pull in pulls:
        pull.start()
    for pull, push in zip(pulls, pushes):
        pull.wait()
        push.start()
    for push in pushes:
        push.wait()


HBM = pl.BlockSpec(memory_space=pltpu.HBM)


def per_device(query, key, value, cotangent, global_ids, rand_owner, rand_local):
    tokens, features = query.shape
    blocks = tokens // BLOCK
    heads = features // HEAD_DIM
    count = lax.axis_size("ctx")
    shares = count // heads
    own_blocks = blocks // shares
    own_tokens = own_blocks * BLOCK
    all_blocks = count * blocks
    entries = count * own_blocks * ROUNDS
    shape = jax.ShapeDtypeStruct
    bf16, f32, i32 = jnp.bfloat16, jnp.float32, jnp.int32

    dma = pltpu.SemaphoreType.DMA((count,))
    flat = shape((tokens, features), bf16)
    whole = pltpu.VMEM((tokens, features), bf16)
    index = (rand_owner.shape[1], all_blocks)
    results = pl.pallas_call(
        functools.partial(fused_kernel, count, shares),
        out_shape=(flat,) * 4,
        in_specs=[HBM] * 7,
        out_specs=(HBM,) * 4,
        scratch_shapes=[
            pltpu.VMEM((heads, tokens, PAIR), bf16),
            pltpu.VMEM((heads, tokens, PAIR), bf16),
            pltpu.VMEM((all_blocks, BLOCK, PAIR), bf16),
            pltpu.VMEM((count, own_tokens, PAIR), bf16),
            pltpu.VMEM((count, own_tokens, PAIR), bf16),
            pltpu.VMEM((count, own_tokens, PAIR), bf16),
            pltpu.VMEM((count, tokens, PAIR), bf16),
            pltpu.VMEM((count, tokens, PAIR), bf16),
            pltpu.VMEM((count * tokens, PAIR), f32),
            pltpu.VMEM((entries + 1, BLOCK, PAIR), f32),
            pltpu.VMEM((1 << GLOBALS, BLOCK, PAIR), f32),
            whole,
            whole,
            whole,
            whole,
            pltpu.VMEM(index, i32),
            pltpu.VMEM(index, i32),
            pltpu.VMEM((2 * ROUNDS + 2, all_blocks), i32),
            pltpu.SMEM((GLOBALS,), i32),
            pltpu.SMEM(index, i32),
            pltpu.SMEM(index, i32),
            pltpu.SMEM((2 * ROUNDS + 2, all_blocks), i32),
            pltpu.SemaphoreType.DMA((10,)),
            pltpu.SemaphoreType.DMA((2, heads // 2)),
        ]
        + [dma] * 8,
        compiler_params=pltpu.CompilerParams(
            collective_id=0, has_side_effects=True, vmem_limit_bytes=60 * 1024 * 1024
        ),
        name="attend",
    )(global_ids, rand_owner.T, rand_local.T, query, key, value, cotangent)
    return pl.pallas_call(
        store_kernel,
        out_shape=(flat,) * 4,
        in_specs=[HBM] * 4,
        out_specs=(HBM,) * 4,
        scratch_shapes=[pltpu.VMEM((4, tokens, features), bf16)]
        + [pltpu.SemaphoreType.DMA((4, 2))] * 2,
        compiler_params=pltpu.CompilerParams(vmem_limit_bytes=60 * 1024 * 1024),
        name="store",
    )(*results)


def solution(mesh):
    rows = P(("groups", "ctx"), None)
    return jax.shard_map(
        per_device,
        mesh=mesh,
        in_specs=(rows, rows, rows, rows, P("groups"), P("groups", None), P("groups", None)),
        out_specs=(rows,) * 4,
        check_vma=False,
    )
```

```python
import functools

import jax
import jax.numpy as jnp
from jax import lax
from jax.experimental import pallas as pl
from jax.experimental.pallas import tpu as pltpu
from jax.sharding import PartitionSpec as P

HEAD_DIM = 64
GROUP_HEADS = 8
BLOCK = 64
GLOBALS = 2
ROUNDS = 3
PAIR = 2 * HEAD_DIM
NEG_FILL = -1e30
SCALE = HEAD_DIM ** (-0.5)
MESH = pl.DeviceIdType.MESH


def lanes_joined(left, right):
    return jnp.concatenate([left, right], axis=1)


def fused_kernel(
    count,
    shares,
    glob_hbm,
    owner_hbm,
    local_hbm,
    q_hbm,
    k_hbm,
    v_hbm,
    d_hbm,
    att_ref,
    gq_ref,
    gk_ref,
    gv_ref,
    kv_pack,
    qd_pack,
    kv_all,
    qd_all,
    qo_put,
    qo_got,
    gkv_put,
    gkv_got,
    acc_ref,
    chain_ref,
    glob_ref,
    q_ref,
    k_ref,
    v_ref,
    d_ref,
    owner_vec,
    local_vec,
    table_vec,
    glob_ids,
    owner_ref,
    local_ref,
    table,
    fetch,
    drain,
    kv_out,
    kv_in,
    qd_out,
    qd_in,
    qo_out,
    qo_in,
    gkv_out,
    gkv_in,
):
    me = lax.axis_index("ctx")
    heads, tokens = kv_pack.shape[:2]
    blocks = tokens // BLOCK
    own_tokens = tokens // shares
    own_blocks = own_tokens // BLOCK
    all_blocks = count * blocks
    entries = count * own_blocks * ROUNDS
    my_share = lax.rem(me, shares)
    my_head = me // shares
    my_group = my_head // GROUP_HEADS
    my_rows = pl.ds(pl.multiple_of(my_share * own_tokens, own_tokens), own_tokens)

    def differ(one, other):
        total, bit = 0, 1
        while bit < count:
            total = total + bit * lax.rem(lax.div(one, bit) + lax.div(other, bit), 2)
            bit *= 2
        return total

    half = count // 2

    def peer_of(step):
        step = jnp.int32(step)
        return differ(me, step // 2 + half * lax.rem(step, 2))

    def step_to(peer):
        gap = differ(me, peer)
        return jnp.where(gap >= half, 2 * (gap - half) + 1, 2 * gap)

    pulls = [
        pltpu.make_async_copy(source, target, fetch.at[index])
        for index, (source, target) in enumerate(
            (
                (k_hbm, k_ref),
                (v_hbm, v_ref),
                (q_hbm, q_ref),
                (d_hbm, d_ref),
                (owner_hbm, owner_ref),
                (local_hbm, local_ref),
                (owner_hbm, owner_vec),
                (local_hbm, local_vec),
                (glob_hbm, glob_ids),
            )
        )
    ]
    for pull in pulls:
        pull.start()
    barrier = pltpu.get_barrier_semaphore()
    for step in range(1, count):
        peer = peer_of(step)
        pl.semaphore_signal(barrier, inc=1, device_id={"ctx": peer}, device_id_type=MESH)

    def pack(left_ref, right_ref, out_ref):
        for pair in range(heads // 2):
            cols = slice(pair * PAIR, (pair + 1) * PAIR)
            left = left_ref[:, cols]
            right = right_ref[:, cols]
            out_ref[2 * pair] = lanes_joined(left[:, :HEAD_DIM], right[:, :HEAD_DIM])
            out_ref[2 * pair + 1] = lanes_joined(left[:, HEAD_DIM:], right[:, HEAD_DIM:])

    pulls[0].wait()
    pulls[1].wait()
    pack(k_ref, v_ref, kv_pack)
    pl.semaphore_wait(barrier, count - 1)

    def kv_copy(dest, came):
        return pltpu.make_async_remote_copy(
            src_ref=kv_pack.at[dest // shares].reshape(blocks, BLOCK, PAIR),
            dst_ref=kv_all.at[pl.ds(came * blocks, blocks)],
            send_sem=kv_out.at[dest],
            recv_sem=kv_in.at[came],
            device_id={"ctx": dest},
            device_id_type=MESH,
        )

    def qd_copy(dest, came):
        start = pl.multiple_of(lax.rem(dest, shares) * own_tokens, own_tokens)
        return pltpu.make_async_remote_copy(
            src_ref=qd_pack.at[dest // shares, pl.ds(start, own_tokens)],
            dst_ref=qd_all.at[came],
            send_sem=qd_out.at[dest],
            recv_sem=qd_in.at[came],
            device_id={"ctx": dest},
            device_id_type=MESH,
        )

    def row_copy(put_ref, got_ref, out_sem, in_sem):
        def copy(dest, came):
            return pltpu.make_async_remote_copy(
                src_ref=put_ref.at[dest],
                dst_ref=got_ref.at[came],
                send_sem=out_sem.at[dest],
                recv_sem=in_sem.at[came],
                device_id={"ctx": dest},
                device_id_type=MESH,
            )

        return copy

    qo_copy = row_copy(qo_put, qo_got, qo_out, qo_in)
    gkv_copy = row_copy(gkv_put, gkv_got, gkv_out, gkv_in)

    for step in range(1, count):
        kv_copy(peer_of(step), me).start()
    pulls[2].wait()
    pulls[3].wait()
    pack(q_ref, d_ref, qd_pack)
    for step in range(1, count):
        qd_copy(peer_of(step), me).start()

    for part in range(blocks):
        kv_all[me * blocks + part] = kv_pack[my_head, part * BLOCK : (part + 1) * BLOCK]
    qd_all[me] = qd_pack[my_head, my_rows, :]
    acc_ref[...] = jnp.zeros_like(acc_ref)
    glob_ref[...] = jnp.zeros_like(glob_ref)
    chain_ref[entries] = jnp.zeros_like(chain_ref[entries])

    for pull in pulls[4:]:
        pull.wait()
    first_row = my_group * ROUNDS
    rows = pl.ds(first_row, ROUNDS)
    places = owner_vec[rows, :] * blocks + local_vec[rows, :]
    block_of = lax.broadcasted_iota(jnp.int32, (ROUNDS, all_blocks), 1)
    round_of = lax.broadcasted_iota(jnp.int32, (ROUNDS, all_blocks), 0)
    turn = step_to(lax.div(block_of, blocks))
    part_of = lax.rem(block_of, blocks) - my_share * own_blocks
    order = (turn * own_blocks + part_of) * ROUNDS + round_of
    order = jnp.where((part_of >= 0) & (part_of < own_blocks), order, -1)
    lane_block = lax.broadcasted_iota(jnp.int32, (1, all_blocks), 1)

    def link(step, carry):
        before, last = carry
        peer = peer_of(step)
        for part in range(own_blocks):
            block = peer * blocks + my_share * own_blocks + part
            for kind in range(ROUNDS):
                entry = (step * own_blocks + part) * ROUNDS + kind
                place = (
                    owner_ref[first_row + kind, block] * blocks + local_ref[first_row + kind, block]
                )
                before = jnp.where((places == place) & (order > entry), entry, before)
                last = jnp.where(lane_block == place, entry, last)
        return before, last

    before, last = lax.fori_loop(
        0,
        count,
        link,
        (
            jnp.full((ROUNDS, all_blocks), entries, jnp.int32),
            jnp.full((1, all_blocks), entries, jnp.int32),
        ),
    )
    which = jnp.zeros((1, all_blocks), jnp.int32)
    for index in range(GLOBALS):
        which += jnp.where(lane_block == glob_ids[index], 1 << index, 0)
    table_vec[0:ROUNDS, :] = places
    table_vec[ROUNDS : 2 * ROUNDS, :] = before
    table_vec[2 * ROUNDS : 2 * ROUNDS + 1, :] = last
    table_vec[2 * ROUNDS + 1 : 2 * ROUNDS + 2, :] = which
    to_scalar = pltpu.make_async_copy(table_vec, table, fetch.at[len(pulls)])
    to_scalar.start()
    to_scalar.wait()

    for step in range(1, count):
        peer = peer_of(step)
        kv_copy(peer, peer).wait_recv()

    lane = lax.broadcasted_iota(jnp.int32, (BLOCK, PAIR), 1)
    low = lane < HEAD_DIM
    row_lane = lax.broadcasted_iota(jnp.int32, (1, PAIR), 1)
    contract_last = (((1,), (1,)), ((), ()))
    contract_first = (((0,), (0,)), ((), ()))

    def load(peer, part):
        block = peer * blocks + my_share * own_blocks + part
        qd = qd_all[peer, part * BLOCK : (part + 1) * BLOCK, :]
        near = [lax.rem(block + all_blocks - 1, all_blocks), lax.rem(block + 1, all_blocks), block]
        spots = near + [glob_ids[kind] for kind in range(GLOBALS)]
        spots = spots + [table[kind, block] for kind in range(ROUNDS)]
        kv = jnp.concatenate([kv_all[p] for p in spots], axis=0)
        zero = jnp.zeros_like(qd)
        diag = jnp.concatenate(
            [jnp.where(low, qd * jnp.bfloat16(SCALE), zero), jnp.where(low, zero, qd)], axis=0
        )
        both = lax.dot_general(diag, kv, contract_last, preferred_element_type=jnp.float32)
        return block, near, qd, kv, diag, both

    def soften(block, both):
        scores = both[:BLOCK]
        bias = jnp.where(
            row_lane < BLOCK,
            jnp.where(block == 0, NEG_FILL, 0.0),
            jnp.where(block == all_blocks - 1, NEG_FILL, 0.0),
        ).astype(jnp.float32)
        scores = lanes_joined(scores[:, :PAIR] + bias, scores[:, PAIR:])
        row_max = jnp.max(scores, axis=1, keepdims=True)
        weights = jnp.exp(scores - row_max)
        probs = weights * (1.0 / jnp.sum(weights, axis=1, keepdims=True))
        return probs, probs.astype(jnp.bfloat16)

    def finish(peer, step, part, block, qd, kv, diag, both, probs, probs_b, attended):
        row_dot = jnp.sum(
            jnp.where(low, 0.0, qd.astype(jnp.float32) * attended.astype(jnp.float32)),
            axis=1,
            keepdims=True,
        )
        dscore = (probs * (both[BLOCK:] - row_dot)).astype(jnp.bfloat16)
        grad_q = jnp.dot(dscore, kv, preferred_element_type=jnp.float32) * SCALE
        qo_put[peer, part * BLOCK : (part + 1) * BLOCK, :] = jnp.where(
            low, grad_q.astype(jnp.bfloat16), attended
        )
        terms = lax.dot_general(
            jnp.concatenate([dscore, probs_b], axis=0),
            diag,
            contract_first,
            preferred_element_type=jnp.float32,
        )
        return terms

    def front(peer, step):
        stage = [load(peer, part) for part in range(own_blocks)]
        soft = [soften(block, both) for block, _, _, _, _, both in stage]
        seen = [
            jnp.dot(probs_b, kept[3], preferred_element_type=jnp.float32).astype(jnp.bfloat16)
            for kept, (_, probs_b) in zip(stage, soft)
        ]
        return [
            (
                block,
                near,
                finish(peer, step, part, block, qd, kv, diag, both, *soft[part], seen[part]),
            )
            for part, (block, near, qd, kv, diag, both) in enumerate(stage)
        ]

    def step_of(step, carry):
        peer = peer_of(step)

        @pl.when(step > 0)
        def _():
            qd_copy(peer, peer).wait_recv()

        done = front(peer, step)
        for part, (block, near, terms) in enumerate(done):
            for kind in range(3):
                spot = pl.ds(pl.multiple_of(near[kind] * BLOCK, BLOCK), BLOCK)
                acc_ref[spot, :] += terms[kind * BLOCK : (kind + 1) * BLOCK]
            for kind in range(ROUNDS):
                start = (3 + GLOBALS + kind) * BLOCK
                term = terms[start : start + BLOCK].astype(jnp.bfloat16).astype(jnp.float32)
                entry = (step * own_blocks + part) * ROUNDS + kind
                chain_ref[entry] = chain_ref[table[ROUNDS + kind, block]] + term
        shared = functools.reduce(
            jnp.add, [terms[3 * BLOCK : (3 + GLOBALS) * BLOCK] for _, _, terms in done]
        )
        for index in range(GLOBALS):
            own = shared[index * BLOCK : (index + 1) * BLOCK]
            for mix in range(1, 1 << GLOBALS):
                if mix >> index & 1:
                    glob_ref[mix] += own

        @pl.when(step > 1)
        def _():
            qo_copy(peer_of(step - 1), me).start()

        return carry

    lax.fori_loop(0, count, step_of, 0)
    qo_copy(peer_of(count - 1), me).start()

    def total_of(step, carry):
        dest = peer_of(step)
        for part in range(blocks):
            block = dest * blocks + part
            spot = pl.ds(pl.multiple_of(block * BLOCK, BLOCK), BLOCK)
            total = acc_ref[spot, :] + chain_ref[table[2 * ROUNDS, block]]
            total = total + glob_ref[table[2 * ROUNDS + 1, block]]
            gkv_put[dest, part * BLOCK : (part + 1) * BLOCK, :] = total.astype(jnp.bfloat16)

        @pl.when(step > 0)
        def _():
            gkv_copy(dest, me).start()

        return carry

    lax.fori_loop(0, count, total_of, 0)
    qo_got[me] = qo_put[me]
    gkv_got[me] = gkv_put[me]

    for step in range(1, count):
        peer = peer_of(step)
        qo_copy(peer, peer).wait_recv()
    for pair in range(heads // 2):
        cols = slice(pair * PAIR, (pair + 1) * PAIR)
        for share in range(shares):
            part = slice(share * own_tokens, (share + 1) * own_tokens)
            even = qo_got[2 * pair * shares + share]
            odd = qo_got[(2 * pair + 1) * shares + share]
            q_ref[part, cols] = lanes_joined(even[:, :HEAD_DIM], odd[:, :HEAD_DIM])
            d_ref[part, cols] = lanes_joined(even[:, HEAD_DIM:], odd[:, HEAD_DIM:])
    pushes = [
        pltpu.make_async_copy(source, target, fetch.at[place])
        for place, (source, target) in enumerate(((q_ref, gq_ref), (d_ref, att_ref)))
    ]
    for push in pushes:
        push.start()
    for step in range(1, count):
        peer = peer_of(step)
        kv_copy(peer, me).wait_send()
        qd_copy(peer, me).wait_send()
        qo_copy(peer, me).wait_send()

    def head_of(head):
        for share in range(shares):
            source = head * shares + share

            @pl.when(source != me)
            def _():
                gkv_copy(source, source).wait_recv()

        total = gkv_got[head * shares]
        if shares > 1:
            total = total.astype(jnp.float32)
            for share in range(1, shares):
                total += gkv_got[head * shares + share].astype(jnp.float32)
            total = total.astype(jnp.bfloat16)
        return total

    for pair in range(heads // 2):
        cols = slice(pair * PAIR, (pair + 1) * PAIR)
        even = head_of(2 * pair)
        odd = head_of(2 * pair + 1)
        k_ref[:, cols] = lanes_joined(even[:, :HEAD_DIM], odd[:, :HEAD_DIM])
        v_ref[:, cols] = lanes_joined(even[:, HEAD_DIM:], odd[:, HEAD_DIM:])
        for place, (source, target) in enumerate(((k_ref, gk_ref), (v_ref, gv_ref))):
            push = pltpu.make_async_copy(
                source.at[:, cols], target.at[:, cols], drain.at[place, pair]
            )
            push.start()
            pushes.append(push)
    for step in range(1, count):
        gkv_copy(peer_of(step), me).wait_send()
    for push in pushes:
        push.wait()


def store_kernel(*refs):
    size = (len(refs) - 3) // 2
    hold, come, go = refs[2 * size :]
    half = hold.shape[1] // 2
    pulls, pushes = [], []
    for index in range(size):
        for part in range(2):
            rows = pl.ds(part * half, half)
            here = hold.at[index, rows]
            pulls.append(pltpu.make_async_copy(refs[index].at[rows], here, come.at[index, part]))
            pushes.append(
                pltpu.make_async_copy(here, refs[size + index].at[rows], go.at[index, part])
            )
    for pull in pulls:
        pull.start()
    for pull, push in zip(pulls, pushes):
        pull.wait()
        push.start()
    for push in pushes:
        push.wait()


HBM = pl.BlockSpec(memory_space=pltpu.HBM)


def per_device(query, key, value, cotangent, global_ids, rand_owner, rand_local):
    tokens, features = query.shape
    blocks = tokens // BLOCK
    heads = features // HEAD_DIM
    count = lax.axis_size("ctx")
    shares = count // heads
    own_blocks = blocks // shares
    own_tokens = own_blocks * BLOCK
    all_blocks = count * blocks
    entries = count * own_blocks * ROUNDS
    shape = jax.ShapeDtypeStruct
    bf16, f32, i32 = jnp.bfloat16, jnp.float32, jnp.int32

    dma = pltpu.SemaphoreType.DMA((count,))
    flat = shape((tokens, features), bf16)
    whole = pltpu.VMEM((tokens, features), bf16)
    index = (rand_owner.shape[1], all_blocks)
    results = pl.pallas_call(
        functools.partial(fused_kernel, count, shares),
        out_shape=(flat,) * 4,
        in_specs=[HBM] * 7,
        out_specs=(HBM,) * 4,
        scratch_shapes=[
            pltpu.VMEM((heads, tokens, PAIR), bf16),
            pltpu.VMEM((heads, tokens, PAIR), bf16),
            pltpu.VMEM((all_blocks, BLOCK, PAIR), bf16),
            pltpu.VMEM((count, own_tokens, PAIR), bf16),
            pltpu.VMEM((count, own_tokens, PAIR), bf16),
            pltpu.VMEM((count, own_tokens, PAIR), bf16),
            pltpu.VMEM((count, tokens, PAIR), bf16),
            pltpu.VMEM((count, tokens, PAIR), bf16),
            pltpu.VMEM((count * tokens, PAIR), f32),
            pltpu.VMEM((entries + 1, BLOCK, PAIR), f32),
            pltpu.VMEM((1 << GLOBALS, BLOCK, PAIR), f32),
            whole,
            whole,
            whole,
            whole,
            pltpu.VMEM(index, i32),
            pltpu.VMEM(index, i32),
            pltpu.VMEM((2 * ROUNDS + 2, all_blocks), i32),
            pltpu.SMEM((GLOBALS,), i32),
            pltpu.SMEM(index, i32),
            pltpu.SMEM(index, i32),
            pltpu.SMEM((2 * ROUNDS + 2, all_blocks), i32),
            pltpu.SemaphoreType.DMA((10,)),
            pltpu.SemaphoreType.DMA((2, heads // 2)),
        ]
        + [dma] * 8,
        compiler_params=pltpu.CompilerParams(
            collective_id=0, has_side_effects=True, vmem_limit_bytes=60 * 1024 * 1024
        ),
        name="attend",
    )(global_ids, rand_owner.T, rand_local.T, query, key, value, cotangent)
    return pl.pallas_call(
        store_kernel,
        out_shape=(flat,) * 4,
        in_specs=[HBM] * 4,
        out_specs=(HBM,) * 4,
        scratch_shapes=[pltpu.VMEM((4, tokens, features), bf16)]
        + [pltpu.SemaphoreType.DMA((4, 2))] * 2,
        compiler_params=pltpu.CompilerParams(vmem_limit_bytes=60 * 1024 * 1024),
        name="store",
    )(*results)


def solution(mesh):
    rows = P(("groups", "ctx"), None)
    return jax.shard_map(
        per_device,
        mesh=mesh,
        in_specs=(rows, rows, rows, rows, P("groups"), P("groups", None), P("groups", None)),
        out_specs=(rows,) * 4,
        check_vma=False,
    )
```

```python
import functools

import jax
import jax.numpy as jnp
from jax import lax
from jax.experimental import pallas as pl
from jax.experimental.pallas import tpu as pltpu
from jax.sharding import PartitionSpec as P

HEAD_DIM = 64
GROUP_HEADS = 8
BLOCK = 64
GLOBALS = 2
ROUNDS = 3
PAIR = 2 * HEAD_DIM
NEG_FILL = -1e30
SCALE = HEAD_DIM ** (-0.5)
MESH = pl.DeviceIdType.MESH


def lanes_joined(left, right):
    return jnp.concatenate([left, right], axis=1)


def fused_kernel(
    count,
    shares,
    glob_hbm,
    owner_hbm,
    local_hbm,
    q_hbm,
    k_hbm,
    v_hbm,
    d_hbm,
    att_ref,
    gq_ref,
    gk_ref,
    gv_ref,
    kv_pack,
    qd_pack,
    kv_all,
    qd_all,
    qo_put,
    qo_got,
    gkv_put,
    gkv_got,
    acc_ref,
    chain_ref,
    glob_ref,
    q_ref,
    k_ref,
    v_ref,
    d_ref,
    owner_vec,
    local_vec,
    table_vec,
    glob_ids,
    owner_ref,
    local_ref,
    table,
    fetch,
    kv_out,
    kv_in,
    qd_out,
    qd_in,
    qo_out,
    qo_in,
    gkv_out,
    gkv_in,
):
    me = lax.axis_index("ctx")
    heads, tokens = kv_pack.shape[:2]
    blocks = tokens // BLOCK
    own_tokens = tokens // shares
    own_blocks = own_tokens // BLOCK
    all_blocks = count * blocks
    entries = count * own_blocks * ROUNDS
    my_share = lax.rem(me, shares)
    my_head = me // shares
    my_group = my_head // GROUP_HEADS
    my_rows = pl.ds(pl.multiple_of(my_share * own_tokens, own_tokens), own_tokens)

    def differ(one, other):
        total, bit = 0, 1
        while bit < count:
            total = total + bit * lax.rem(lax.div(one, bit) + lax.div(other, bit), 2)
            bit *= 2
        return total

    half = count // 2

    def peer_of(step):
        step = jnp.int32(step)
        return differ(me, step // 2 + half * lax.rem(step, 2))

    def step_to(peer):
        gap = differ(me, peer)
        return jnp.where(gap >= half, 2 * (gap - half) + 1, 2 * gap)

    pulls = [
        pltpu.make_async_copy(source, target, fetch.at[index])
        for index, (source, target) in enumerate(
            (
                (k_hbm, k_ref),
                (v_hbm, v_ref),
                (q_hbm, q_ref),
                (d_hbm, d_ref),
                (owner_hbm, owner_ref),
                (local_hbm, local_ref),
                (owner_hbm, owner_vec),
                (local_hbm, local_vec),
                (glob_hbm, glob_ids),
            )
        )
    ]
    for pull in pulls:
        pull.start()
    barrier = pltpu.get_barrier_semaphore()
    for step in range(1, count):
        peer = peer_of(step)
        pl.semaphore_signal(barrier, inc=1, device_id={"ctx": peer}, device_id_type=MESH)

    def pack(left_ref, right_ref, out_ref):
        for pair in range(heads // 2):
            cols = slice(pair * PAIR, (pair + 1) * PAIR)
            left = left_ref[:, cols]
            right = right_ref[:, cols]
            out_ref[2 * pair] = lanes_joined(left[:, :HEAD_DIM], right[:, :HEAD_DIM])
            out_ref[2 * pair + 1] = lanes_joined(left[:, HEAD_DIM:], right[:, HEAD_DIM:])

    pulls[0].wait()
    pulls[1].wait()
    pack(k_ref, v_ref, kv_pack)
    pl.semaphore_wait(barrier, count - 1)

    def kv_copy(dest, came):
        return pltpu.make_async_remote_copy(
            src_ref=kv_pack.at[dest // shares].reshape(blocks, BLOCK, PAIR),
            dst_ref=kv_all.at[pl.ds(came * blocks, blocks)],
            send_sem=kv_out.at[dest],
            recv_sem=kv_in.at[came],
            device_id={"ctx": dest},
            device_id_type=MESH,
        )

    def qd_copy(dest, came):
        start = pl.multiple_of(lax.rem(dest, shares) * own_tokens, own_tokens)
        return pltpu.make_async_remote_copy(
            src_ref=qd_pack.at[dest // shares, pl.ds(start, own_tokens)],
            dst_ref=qd_all.at[came],
            send_sem=qd_out.at[dest],
            recv_sem=qd_in.at[came],
            device_id={"ctx": dest},
            device_id_type=MESH,
        )

    def row_copy(put_ref, got_ref, out_sem, in_sem):
        def copy(dest, came):
            return pltpu.make_async_remote_copy(
                src_ref=put_ref.at[dest],
                dst_ref=got_ref.at[came],
                send_sem=out_sem.at[dest],
                recv_sem=in_sem.at[came],
                device_id={"ctx": dest},
                device_id_type=MESH,
            )

        return copy

    qo_copy = row_copy(qo_put, qo_got, qo_out, qo_in)
    gkv_copy = row_copy(gkv_put, gkv_got, gkv_out, gkv_in)

    for step in range(1, count):
        kv_copy(peer_of(step), me).start()
    pulls[2].wait()
    pulls[3].wait()
    pack(q_ref, d_ref, qd_pack)
    for step in range(1, count):
        qd_copy(peer_of(step), me).start()

    for part in range(blocks):
        kv_all[me * blocks + part] = kv_pack[my_head, part * BLOCK : (part + 1) * BLOCK]
    qd_all[me] = qd_pack[my_head, my_rows, :]
    acc_ref[...] = jnp.zeros_like(acc_ref)
    glob_ref[...] = jnp.zeros_like(glob_ref)
    chain_ref[entries] = jnp.zeros_like(chain_ref[entries])

    for pull in pulls[4:]:
        pull.wait()
    first_row = my_group * ROUNDS
    rows = pl.ds(first_row, ROUNDS)
    places = owner_vec[rows, :] * blocks + local_vec[rows, :]
    block_of = lax.broadcasted_iota(jnp.int32, (ROUNDS, all_blocks), 1)
    round_of = lax.broadcasted_iota(jnp.int32, (ROUNDS, all_blocks), 0)
    turn = step_to(lax.div(block_of, blocks))
    part_of = lax.rem(block_of, blocks) - my_share * own_blocks
    order = (turn * own_blocks + part_of) * ROUNDS + round_of
    order = jnp.where((part_of >= 0) & (part_of < own_blocks), order, -1)
    lane_block = lax.broadcasted_iota(jnp.int32, (1, all_blocks), 1)

    def link(step, carry):
        before, last = carry
        peer = peer_of(step)
        for part in range(own_blocks):
            block = peer * blocks + my_share * own_blocks + part
            for kind in range(ROUNDS):
                entry = (step * own_blocks + part) * ROUNDS + kind
                place = (
                    owner_ref[first_row + kind, block] * blocks + local_ref[first_row + kind, block]
                )
                before = jnp.where((places == place) & (order > entry), entry, before)
                last = jnp.where(lane_block == place, entry, last)
        return before, last

    before, last = lax.fori_loop(
        0,
        count,
        link,
        (
            jnp.full((ROUNDS, all_blocks), entries, jnp.int32),
            jnp.full((1, all_blocks), entries, jnp.int32),
        ),
    )
    which = jnp.zeros((1, all_blocks), jnp.int32)
    for index in range(GLOBALS):
        which += jnp.where(lane_block == glob_ids[index], 1 << index, 0)
    table_vec[0:ROUNDS, :] = places
    table_vec[ROUNDS : 2 * ROUNDS, :] = before
    table_vec[2 * ROUNDS : 2 * ROUNDS + 1, :] = last
    table_vec[2 * ROUNDS + 1 : 2 * ROUNDS + 2, :] = which
    to_scalar = pltpu.make_async_copy(table_vec, table, fetch.at[len(pulls)])
    to_scalar.start()
    to_scalar.wait()

    for step in range(1, count):
        peer = peer_of(step)
        kv_copy(peer, peer).wait_recv()

    lane = lax.broadcasted_iota(jnp.int32, (BLOCK, PAIR), 1)
    low = lane < HEAD_DIM
    row_lane = lax.broadcasted_iota(jnp.int32, (1, PAIR), 1)
    contract_last = (((1,), (1,)), ((), ()))
    contract_first = (((0,), (0,)), ((), ()))

    def load(peer, part):
        block = peer * blocks + my_share * own_blocks + part
        qd = qd_all[peer, part * BLOCK : (part + 1) * BLOCK, :]
        near = [lax.rem(block + all_blocks - 1, all_blocks), lax.rem(block + 1, all_blocks), block]
        spots = near + [glob_ids[kind] for kind in range(GLOBALS)]
        spots = spots + [table[kind, block] for kind in range(ROUNDS)]
        kv = jnp.concatenate([kv_all[p] for p in spots], axis=0)
        zero = jnp.zeros_like(qd)
        diag = jnp.concatenate(
            [jnp.where(low, qd * jnp.bfloat16(SCALE), zero), jnp.where(low, zero, qd)], axis=0
        )
        both = lax.dot_general(diag, kv, contract_last, preferred_element_type=jnp.float32)
        return block, near, qd, kv, diag, both

    def soften(block, both):
        scores = both[:BLOCK]
        bias = jnp.where(
            row_lane < BLOCK,
            jnp.where(block == 0, NEG_FILL, 0.0),
            jnp.where(block == all_blocks - 1, NEG_FILL, 0.0),
        ).astype(jnp.float32)
        scores = lanes_joined(scores[:, :PAIR] + bias, scores[:, PAIR:])
        row_max = jnp.max(scores, axis=1, keepdims=True)
        weights = jnp.exp(scores - row_max)
        probs = weights * (1.0 / jnp.sum(weights, axis=1, keepdims=True))
        return probs, probs.astype(jnp.bfloat16)

    def finish(peer, step, part, block, qd, kv, diag, both, probs, probs_b, attended):
        row_dot = jnp.sum(
            jnp.where(low, 0.0, qd.astype(jnp.float32) * attended.astype(jnp.float32)),
            axis=1,
            keepdims=True,
        )
        dscore = (probs * (both[BLOCK:] - row_dot)).astype(jnp.bfloat16)
        grad_q = jnp.dot(dscore, kv, preferred_element_type=jnp.float32) * SCALE
        qo_put[peer, part * BLOCK : (part + 1) * BLOCK, :] = jnp.where(
            low, grad_q.astype(jnp.bfloat16), attended
        )
        terms = lax.dot_general(
            jnp.concatenate([dscore, probs_b], axis=0),
            diag,
            contract_first,
            preferred_element_type=jnp.float32,
        )
        return terms

    def front(peer, step):
        stage = [load(peer, part) for part in range(own_blocks)]
        soft = [soften(block, both) for block, _, _, _, _, both in stage]
        seen = [
            jnp.dot(probs_b, kept[3], preferred_element_type=jnp.float32).astype(jnp.bfloat16)
            for kept, (_, probs_b) in zip(stage, soft)
        ]
        return [
            (
                block,
                near,
                finish(peer, step, part, block, qd, kv, diag, both, *soft[part], seen[part]),
            )
            for part, (block, near, qd, kv, diag, both) in enumerate(stage)
        ]

    def step_of(step, carry):
        peer = peer_of(step)

        @pl.when(step > 0)
        def _():
            qd_copy(peer, peer).wait_recv()

        done = front(peer, step)
        for part, (block, near, terms) in enumerate(done):
            for kind in range(3):
                spot = pl.ds(pl.multiple_of(near[kind] * BLOCK, BLOCK), BLOCK)
                acc_ref[spot, :] += terms[kind * BLOCK : (kind + 1) * BLOCK]
            for kind in range(ROUNDS):
                start = (3 + GLOBALS + kind) * BLOCK
                term = terms[start : start + BLOCK].astype(jnp.bfloat16).astype(jnp.float32)
                entry = (step * own_blocks + part) * ROUNDS + kind
                chain_ref[entry] = chain_ref[table[ROUNDS + kind, block]] + term
        shared = functools.reduce(
            jnp.add, [terms[3 * BLOCK : (3 + GLOBALS) * BLOCK] for _, _, terms in done]
        )
        for index in range(GLOBALS):
            own = shared[index * BLOCK : (index + 1) * BLOCK]
            for mix in range(1, 1 << GLOBALS):
                if mix >> index & 1:
                    glob_ref[mix] += own

        @pl.when(step > 1)
        def _():
            qo_copy(peer_of(step - 1), me).start()

        return carry

    lax.fori_loop(0, count, step_of, 0)
    qo_copy(peer_of(count - 1), me).start()

    def total_of(step, carry):
        dest = peer_of(step)
        for part in range(blocks):
            block = dest * blocks + part
            spot = pl.ds(pl.multiple_of(block * BLOCK, BLOCK), BLOCK)
            total = acc_ref[spot, :] + chain_ref[table[2 * ROUNDS, block]]
            total = total + glob_ref[table[2 * ROUNDS + 1, block]]
            gkv_put[dest, part * BLOCK : (part + 1) * BLOCK, :] = total.astype(jnp.bfloat16)

        @pl.when(step > 0)
        def _():
            gkv_copy(dest, me).start()

        return carry

    lax.fori_loop(0, count, total_of, 0)
    qo_got[me] = qo_put[me]
    gkv_got[me] = gkv_put[me]

    for step in range(1, count):
        peer = peer_of(step)
        qo_copy(peer, peer).wait_recv()
    for pair in range(heads // 2):
        cols = slice(pair * PAIR, (pair + 1) * PAIR)
        for share in range(shares):
            part = slice(share * own_tokens, (share + 1) * own_tokens)
            even = qo_got[2 * pair * shares + share]
            odd = qo_got[(2 * pair + 1) * shares + share]
            gq_ref[part, cols] = lanes_joined(even[:, :HEAD_DIM], odd[:, :HEAD_DIM])
            att_ref[part, cols] = lanes_joined(even[:, HEAD_DIM:], odd[:, HEAD_DIM:])
    for step in range(1, count):
        peer = peer_of(step)
        kv_copy(peer, me).wait_send()
        qd_copy(peer, me).wait_send()
        qo_copy(peer, me).wait_send()

    def head_of(head):
        for share in range(shares):
            source = head * shares + share

            @pl.when(source != me)
            def _():
                gkv_copy(source, source).wait_recv()

        total = gkv_got[head * shares]
        if shares > 1:
            total = total.astype(jnp.float32)
            for share in range(1, shares):
                total += gkv_got[head * shares + share].astype(jnp.float32)
            total = total.astype(jnp.bfloat16)
        return total

    for pair in range(heads // 2):
        cols = slice(pair * PAIR, (pair + 1) * PAIR)
        even = head_of(2 * pair)
        odd = head_of(2 * pair + 1)
        gk_ref[:, cols] = lanes_joined(even[:, :HEAD_DIM], odd[:, :HEAD_DIM])
        gv_ref[:, cols] = lanes_joined(even[:, HEAD_DIM:], odd[:, HEAD_DIM:])
    for step in range(1, count):
        gkv_copy(peer_of(step), me).wait_send()


def store_kernel(*refs):
    size = (len(refs) - 1) // 2
    pushes = [
        pltpu.make_async_copy(refs[index], refs[size + index], refs[-1].at[index])
        for index in range(size)
    ]
    for push in pushes:
        push.start()
    for push in pushes:
        push.wait()


VMEM = pl.BlockSpec(memory_space=pltpu.VMEM)
HBM = pl.BlockSpec(memory_space=pltpu.HBM)


def per_device(query, key, value, cotangent, global_ids, rand_owner, rand_local):
    tokens, features = query.shape
    blocks = tokens // BLOCK
    heads = features // HEAD_DIM
    count = lax.axis_size("ctx")
    shares = count // heads
    own_blocks = blocks // shares
    own_tokens = own_blocks * BLOCK
    all_blocks = count * blocks
    entries = count * own_blocks * ROUNDS
    shape = jax.ShapeDtypeStruct
    bf16, f32, i32 = jnp.bfloat16, jnp.float32, jnp.int32

    operands = [
        pltpu.with_memory_space_constraint(operand, pltpu.HBM)
        for operand in (global_ids, rand_owner.T, rand_local.T, query, key, value, cotangent)
    ]
    dma = pltpu.SemaphoreType.DMA((count,))
    flat = shape((tokens, features), bf16)
    whole = pltpu.VMEM((tokens, features), bf16)
    index = (rand_owner.shape[1], all_blocks)
    results = pl.pallas_call(
        functools.partial(fused_kernel, count, shares),
        out_shape=(flat,) * 4,
        in_specs=[HBM] * 7,
        out_specs=(VMEM,) * 4,
        scratch_shapes=[
            pltpu.VMEM((heads, tokens, PAIR), bf16),
            pltpu.VMEM((heads, tokens, PAIR), bf16),
            pltpu.VMEM((all_blocks, BLOCK, PAIR), bf16),
            pltpu.VMEM((count, own_tokens, PAIR), bf16),
            pltpu.VMEM((count, own_tokens, PAIR), bf16),
            pltpu.VMEM((count, own_tokens, PAIR), bf16),
            pltpu.VMEM((count, tokens, PAIR), bf16),
            pltpu.VMEM((count, tokens, PAIR), bf16),
            pltpu.VMEM((count * tokens, PAIR), f32),
            pltpu.VMEM((entries + 1, BLOCK, PAIR), f32),
            pltpu.VMEM((1 << GLOBALS, BLOCK, PAIR), f32),
            whole,
            whole,
            whole,
            whole,
            pltpu.VMEM(index, i32),
            pltpu.VMEM(index, i32),
            pltpu.VMEM((2 * ROUNDS + 2, all_blocks), i32),
            pltpu.SMEM((GLOBALS,), i32),
            pltpu.SMEM(index, i32),
            pltpu.SMEM(index, i32),
            pltpu.SMEM((2 * ROUNDS + 2, all_blocks), i32),
            pltpu.SemaphoreType.DMA((10,)),
        ]
        + [dma] * 8,
        compiler_params=pltpu.CompilerParams(
            collective_id=0, has_side_effects=True, vmem_limit_bytes=44 * 1024 * 1024
        ),
        name="attend",
    )(*operands)
    return pl.pallas_call(
        store_kernel,
        out_shape=(flat,) * 4,
        in_specs=[VMEM] * 4,
        out_specs=(HBM,) * 4,
        scratch_shapes=[pltpu.SemaphoreType.DMA((4,))],
        compiler_params=pltpu.CompilerParams(vmem_limit_bytes=1024 * 1024),
        name="store",
    )(*results)


def solution(mesh):
    rows = P(("groups", "ctx"), None)
    return jax.shard_map(
        per_device,
        mesh=mesh,
        in_specs=(rows, rows, rows, rows, P("groups"), P("groups", None), P("groups", None)),
        out_specs=(rows,) * 4,
        check_vma=False,
    )
```

```python
import functools

import jax
import jax.numpy as jnp
from jax import lax
from jax.experimental import pallas as pl
from jax.experimental.pallas import tpu as pltpu
from jax.sharding import PartitionSpec as P

HEAD_DIM = 64
GROUP_HEADS = 8
BLOCK = 64
GLOBALS = 2
ROUNDS = 3
PAIR = 2 * HEAD_DIM
NEG_FILL = -1e30
SCALE = HEAD_DIM ** (-0.5)
MESH = pl.DeviceIdType.MESH


def lanes_joined(left, right):
    return jnp.concatenate([left, right], axis=1)


def fused_kernel(
    count,
    shares,
    glob_hbm,
    owner_hbm,
    local_hbm,
    q_hbm,
    k_hbm,
    v_hbm,
    d_hbm,
    att_ref,
    gq_ref,
    gk_ref,
    gv_ref,
    kv_pack,
    qd_pack,
    kv_all,
    qd_all,
    qo_put,
    qo_got,
    gkv_put,
    gkv_got,
    acc_ref,
    chain_ref,
    glob_ref,
    q_ref,
    k_ref,
    v_ref,
    d_ref,
    owner_vec,
    local_vec,
    table_vec,
    glob_ids,
    owner_ref,
    local_ref,
    table,
    fetch,
    ready,
    kv_out,
    kv_in,
    qd_out,
    qd_in,
    qo_out,
    qo_in,
    gkv_out,
    gkv_in,
):
    me = lax.axis_index("ctx")
    heads, tokens = kv_pack.shape[:2]
    blocks = tokens // BLOCK
    own_tokens = tokens // shares
    own_blocks = own_tokens // BLOCK
    all_blocks = count * blocks
    entries = count * own_blocks * ROUNDS
    my_share = lax.rem(me, shares)
    my_head = me // shares
    my_group = my_head // GROUP_HEADS
    my_rows = pl.ds(pl.multiple_of(my_share * own_tokens, own_tokens), own_tokens)

    def differ(one, other):
        total, bit = 0, 1
        while bit < count:
            total = total + bit * lax.rem(lax.div(one, bit) + lax.div(other, bit), 2)
            bit *= 2
        return total

    half = count // 2

    def peer_of(step):
        step = jnp.int32(step)
        return differ(me, step // 2 + half * lax.rem(step, 2))

    def step_to(peer):
        gap = differ(me, peer)
        return jnp.where(gap >= half, 2 * (gap - half) + 1, 2 * gap)

    quarter = count // 4
    my_quarter = me // quarter
    inner = lax.rem(my_quarter + my_quarter // 2, 2)
    same = [*range(3 * quarter, count), *range(1, quarter)]
    unlike = [*range(quarter, 3 * quarter)]
    far = [*range(3 * quarter, count)]
    mixed = [half * (step % 2) + step // 2 for step in range(1, count)]
    width = k_ref.shape[2]

    pulls = []

    def pull(source, target):
        copy = pltpu.make_async_copy(source, target, fetch.at[len(pulls)])
        copy.start()
        pulls.append(copy)

    pieces = [differ(my_quarter, jnp.int32(gap)) for gap in (3, 2, 0, 1)]
    for piece in pieces:
        cols = pl.ds(pl.multiple_of(piece * width, width), width)
        pull(k_hbm.at[:, cols], k_ref.at[piece])
        pull(v_hbm.at[:, cols], v_ref.at[piece])
    barrier = pltpu.get_barrier_semaphore()

    def greet(semaphore, gap):
        pl.semaphore_signal(
            semaphore, inc=1, device_id={"ctx": differ(me, jnp.int32(gap))}, device_id_type=MESH
        )

    for gap in same:
        greet(barrier, gap)

    @pl.when(inner == 1)
    def _():
        for gap in unlike:
            greet(barrier, gap)

    pull(q_hbm, q_ref)
    pull(d_hbm, d_ref)
    pull(owner_hbm, owner_ref)
    pull(local_hbm, local_ref)
    pull(owner_hbm, owner_vec)
    pull(local_hbm, local_vec)
    pull(glob_hbm, glob_ids)

    def pack(left, right, out_ref, head):
        out_ref[head] = lanes_joined(left[:, :HEAD_DIM], right[:, :HEAD_DIM])
        out_ref[head + 1] = lanes_joined(left[:, HEAD_DIM:], right[:, HEAD_DIM:])

    def pack_kv(index):
        pulls[2 * index].wait()
        pulls[2 * index + 1].wait()
        piece = pieces[index]
        for pair in range(heads // 8):
            cols = slice(pair * PAIR, (pair + 1) * PAIR)
            head = piece * (heads // 4) + 2 * pair
            pack(k_ref[piece, :, cols], v_ref[piece, :, cols], kv_pack, head)

    pack_kv(0)

    @pl.when(inner == 0)
    def _():
        for index in range(1, 4):
            pack_kv(index)

    pl.semaphore_wait(barrier, 2 * quarter - 1 + (1 - inner) * 2 * quarter)

    def kv_copy(dest, came):
        return pltpu.make_async_remote_copy(
            src_ref=kv_pack.at[dest // shares].reshape(blocks, BLOCK, PAIR),
            dst_ref=kv_all.at[pl.ds(came * blocks, blocks)],
            send_sem=kv_out.at[dest],
            recv_sem=kv_in.at[came],
            device_id={"ctx": dest},
            device_id_type=MESH,
        )

    def qd_copy(dest, came):
        start = pl.multiple_of(lax.rem(dest, shares) * own_tokens, own_tokens)
        return pltpu.make_async_remote_copy(
            src_ref=qd_pack.at[dest // shares, pl.ds(start, own_tokens)],
            dst_ref=qd_all.at[came],
            send_sem=qd_out.at[dest],
            recv_sem=qd_in.at[came],
            device_id={"ctx": dest},
            device_id_type=MESH,
        )

    def row_copy(put_ref, got_ref, out_sem, in_sem):
        def copy(dest, came):
            return pltpu.make_async_remote_copy(
                src_ref=put_ref.at[dest],
                dst_ref=got_ref.at[came],
                send_sem=out_sem.at[dest],
                recv_sem=in_sem.at[came],
                device_id={"ctx": dest},
                device_id_type=MESH,
            )

        return copy

    qo_copy = row_copy(qo_put, qo_got, qo_out, qo_in)
    gkv_copy = row_copy(gkv_put, gkv_got, gkv_out, gkv_in)

    def feed(gaps):
        for gap in gaps:
            kv_copy(differ(me, jnp.int32(gap)), me).start()

    @pl.when(inner == 0)
    def _():
        for gap in unlike:
            greet(ready, gap)
        feed(mixed)

    @pl.when(inner == 1)
    def _():
        feed(far)
        for index in range(1, 4):
            pack_kv(index)
        pl.semaphore_wait(ready, 2 * quarter)
        feed([gap for gap in mixed if gap not in far])

    pulls[8].wait()
    pulls[9].wait()
    for pair in range(heads // 2):
        cols = slice(pair * PAIR, (pair + 1) * PAIR)
        pack(q_ref[:, cols], d_ref[:, cols], qd_pack, 2 * pair)
    for step in range(1, count):
        qd_copy(peer_of(step), me).start()

    for part in range(blocks):
        kv_all[me * blocks + part] = kv_pack[my_head, part * BLOCK : (part + 1) * BLOCK]
    qd_all[me] = qd_pack[my_head, my_rows, :]
    acc_ref[...] = jnp.zeros_like(acc_ref)
    glob_ref[...] = jnp.zeros_like(glob_ref)
    chain_ref[entries] = jnp.zeros_like(chain_ref[entries])

    for copy in pulls[10:]:
        copy.wait()
    first_row = my_group * ROUNDS
    rows = pl.ds(first_row, ROUNDS)
    places = owner_vec[rows, :] * blocks + local_vec[rows, :]
    block_of = lax.broadcasted_iota(jnp.int32, (ROUNDS, all_blocks), 1)
    round_of = lax.broadcasted_iota(jnp.int32, (ROUNDS, all_blocks), 0)
    turn = step_to(lax.div(block_of, blocks))
    part_of = lax.rem(block_of, blocks) - my_share * own_blocks
    order = (turn * own_blocks + part_of) * ROUNDS + round_of
    order = jnp.where((part_of >= 0) & (part_of < own_blocks), order, -1)
    lane_block = lax.broadcasted_iota(jnp.int32, (1, all_blocks), 1)

    def link(step, carry):
        before, last = carry
        peer = peer_of(step)
        for part in range(own_blocks):
            block = peer * blocks + my_share * own_blocks + part
            for kind in range(ROUNDS):
                entry = (step * own_blocks + part) * ROUNDS + kind
                place = (
                    owner_ref[first_row + kind, block] * blocks + local_ref[first_row + kind, block]
                )
                before = jnp.where((places == place) & (order > entry), entry, before)
                last = jnp.where(lane_block == place, entry, last)
        return before, last

    before, last = lax.fori_loop(
        0,
        count,
        link,
        (
            jnp.full((ROUNDS, all_blocks), entries, jnp.int32),
            jnp.full((1, all_blocks), entries, jnp.int32),
        ),
    )
    which = jnp.zeros((1, all_blocks), jnp.int32)
    for index in range(GLOBALS):
        which += jnp.where(lane_block == glob_ids[index], 1 << index, 0)
    table_vec[0:ROUNDS, :] = places
    table_vec[ROUNDS : 2 * ROUNDS, :] = before
    table_vec[2 * ROUNDS : 2 * ROUNDS + 1, :] = last
    table_vec[2 * ROUNDS + 1 : 2 * ROUNDS + 2, :] = which
    to_scalar = pltpu.make_async_copy(table_vec, table, fetch.at[len(pulls)])
    to_scalar.start()
    to_scalar.wait()

    for step in range(1, count):
        peer = peer_of(step)
        kv_copy(peer, peer).wait_recv()

    lane = lax.broadcasted_iota(jnp.int32, (BLOCK, PAIR), 1)
    low = lane < HEAD_DIM
    row_lane = lax.broadcasted_iota(jnp.int32, (1, PAIR), 1)
    contract_last = (((1,), (1,)), ((), ()))
    contract_first = (((0,), (0,)), ((), ()))

    def load(peer, part):
        block = peer * blocks + my_share * own_blocks + part
        qd = qd_all[peer, part * BLOCK : (part + 1) * BLOCK, :]
        near = [lax.rem(block + all_blocks - 1, all_blocks), lax.rem(block + 1, all_blocks), block]
        spots = near + [glob_ids[kind] for kind in range(GLOBALS)]
        spots = spots + [table[kind, block] for kind in range(ROUNDS)]
        kv = jnp.concatenate([kv_all[p] for p in spots], axis=0)
        zero = jnp.zeros_like(qd)
        diag = jnp.concatenate(
            [jnp.where(low, qd * jnp.bfloat16(SCALE), zero), jnp.where(low, zero, qd)], axis=0
        )
        both = lax.dot_general(diag, kv, contract_last, preferred_element_type=jnp.float32)
        return block, near, qd, kv, diag, both

    def soften(block, both):
        scores = both[:BLOCK]
        bias = jnp.where(
            row_lane < BLOCK,
            jnp.where(block == 0, NEG_FILL, 0.0),
            jnp.where(block == all_blocks - 1, NEG_FILL, 0.0),
        ).astype(jnp.float32)
        scores = lanes_joined(scores[:, :PAIR] + bias, scores[:, PAIR:])
        row_max = jnp.max(scores, axis=1, keepdims=True)
        weights = jnp.exp(scores - row_max)
        probs = weights * (1.0 / jnp.sum(weights, axis=1, keepdims=True))
        return probs, probs.astype(jnp.bfloat16)

    def finish(peer, step, part, block, qd, kv, diag, both, probs, probs_b, attended):
        row_dot = jnp.sum(
            jnp.where(low, 0.0, qd.astype(jnp.float32) * attended.astype(jnp.float32)),
            axis=1,
            keepdims=True,
        )
        dscore = (probs * (both[BLOCK:] - row_dot)).astype(jnp.bfloat16)
        grad_q = jnp.dot(dscore, kv, preferred_element_type=jnp.float32) * SCALE
        qo_put[peer, part * BLOCK : (part + 1) * BLOCK, :] = jnp.where(
            low, grad_q.astype(jnp.bfloat16), attended
        )
        terms = lax.dot_general(
            jnp.concatenate([dscore, probs_b], axis=0),
            diag,
            contract_first,
            preferred_element_type=jnp.float32,
        )
        return terms

    def front(peer, step):
        stage = [load(peer, part) for part in range(own_blocks)]
        soft = [soften(block, both) for block, _, _, _, _, both in stage]
        seen = [
            jnp.dot(probs_b, kept[3], preferred_element_type=jnp.float32).astype(jnp.bfloat16)
            for kept, (_, probs_b) in zip(stage, soft)
        ]
        return [
            (
                block,
                near,
                finish(peer, step, part, block, qd, kv, diag, both, *soft[part], seen[part]),
            )
            for part, (block, near, qd, kv, diag, both) in enumerate(stage)
        ]

    def step_of(step, carry):
        peer = peer_of(step)

        @pl.when(step > 0)
        def _():
            qd_copy(peer, peer).wait_recv()

        done = front(peer, step)
        for part, (block, near, terms) in enumerate(done):
            for kind in range(3):
                spot = pl.ds(pl.multiple_of(near[kind] * BLOCK, BLOCK), BLOCK)
                acc_ref[spot, :] += terms[kind * BLOCK : (kind + 1) * BLOCK]
            for kind in range(ROUNDS):
                start = (3 + GLOBALS + kind) * BLOCK
                term = terms[start : start + BLOCK].astype(jnp.bfloat16).astype(jnp.float32)
                entry = (step * own_blocks + part) * ROUNDS + kind
                chain_ref[entry] = chain_ref[table[ROUNDS + kind, block]] + term
        shared = functools.reduce(
            jnp.add, [terms[3 * BLOCK : (3 + GLOBALS) * BLOCK] for _, _, terms in done]
        )
        for index in range(GLOBALS):
            own = shared[index * BLOCK : (index + 1) * BLOCK]
            for mix in range(1, 1 << GLOBALS):
                if mix >> index & 1:
                    glob_ref[mix] += own

        @pl.when(step > 1)
        def _():
            qo_copy(peer_of(step - 1), me).start()

        return carry

    lax.fori_loop(0, count, step_of, 0)
    qo_copy(peer_of(count - 1), me).start()

    def total_of(step, carry):
        dest = peer_of(step)
        for part in range(blocks):
            block = dest * blocks + part
            spot = pl.ds(pl.multiple_of(block * BLOCK, BLOCK), BLOCK)
            total = acc_ref[spot, :] + chain_ref[table[2 * ROUNDS, block]]
            total = total + glob_ref[table[2 * ROUNDS + 1, block]]
            gkv_put[dest, part * BLOCK : (part + 1) * BLOCK, :] = total.astype(jnp.bfloat16)

        @pl.when(step > 0)
        def _():
            gkv_copy(dest, me).start()

        return carry

    lax.fori_loop(0, count, total_of, 0)
    qo_got[me] = qo_put[me]
    gkv_got[me] = gkv_put[me]

    for step in range(1, count):
        peer = peer_of(step)
        qo_copy(peer, peer).wait_recv()
    for pair in range(heads // 2):
        cols = slice(pair * PAIR, (pair + 1) * PAIR)
        for share in range(shares):
            part = slice(share * own_tokens, (share + 1) * own_tokens)
            even = qo_got[2 * pair * shares + share]
            odd = qo_got[(2 * pair + 1) * shares + share]
            gq_ref[part, cols] = lanes_joined(even[:, :HEAD_DIM], odd[:, :HEAD_DIM])
            att_ref[part, cols] = lanes_joined(even[:, HEAD_DIM:], odd[:, HEAD_DIM:])
    for step in range(1, count):
        peer = peer_of(step)
        kv_copy(peer, me).wait_send()
        qd_copy(peer, me).wait_send()
        qo_copy(peer, me).wait_send()

    def head_of(head):
        for share in range(shares):
            source = head * shares + share

            @pl.when(source != me)
            def _():
                gkv_copy(source, source).wait_recv()

        total = gkv_got[head * shares]
        if shares > 1:
            total = total.astype(jnp.float32)
            for share in range(1, shares):
                total += gkv_got[head * shares + share].astype(jnp.float32)
            total = total.astype(jnp.bfloat16)
        return total

    for gap in range(heads // 2):
        if gap == heads // 2 - 1:
            for step in range(1, count):
                gkv_copy(peer_of(step), me).wait_send()
        pair = differ(my_head // 2, jnp.int32(gap))
        cols = pl.ds(pl.multiple_of(pair * PAIR, PAIR), PAIR)
        even = head_of(2 * pair)
        odd = head_of(2 * pair + 1)
        gk_ref[:, cols] = lanes_joined(even[:, :HEAD_DIM], odd[:, :HEAD_DIM])
        gv_ref[:, cols] = lanes_joined(even[:, HEAD_DIM:], odd[:, HEAD_DIM:])


def store_kernel(*refs):
    size = (len(refs) - 1) // 2
    pushes = [
        pltpu.make_async_copy(refs[index], refs[size + index], refs[-1].at[index])
        for index in range(size)
    ]
    for push in pushes:
        push.start()
    for push in pushes:
        push.wait()


VMEM = pl.BlockSpec(memory_space=pltpu.VMEM)
HBM = pl.BlockSpec(memory_space=pltpu.HBM)


def per_device(query, key, value, cotangent, global_ids, rand_owner, rand_local):
    tokens, features = query.shape
    blocks = tokens // BLOCK
    heads = features // HEAD_DIM
    count = lax.axis_size("ctx")
    shares = count // heads
    own_blocks = blocks // shares
    own_tokens = own_blocks * BLOCK
    all_blocks = count * blocks
    entries = count * own_blocks * ROUNDS
    shape = jax.ShapeDtypeStruct
    bf16, f32, i32 = jnp.bfloat16, jnp.float32, jnp.int32

    operands = [
        pltpu.with_memory_space_constraint(operand, pltpu.HBM)
        for operand in (global_ids, rand_owner.T, rand_local.T, query, key, value, cotangent)
    ]
    dma = pltpu.SemaphoreType.DMA((count,))
    flat = shape((tokens, features), bf16)
    whole = pltpu.VMEM((tokens, features), bf16)
    cut = pltpu.VMEM((4, tokens, features // 4), bf16)
    index = (rand_owner.shape[1], all_blocks)
    results = pl.pallas_call(
        functools.partial(fused_kernel, count, shares),
        out_shape=(flat,) * 4,
        in_specs=[HBM] * 7,
        out_specs=(VMEM,) * 4,
        scratch_shapes=[
            pltpu.VMEM((heads, tokens, PAIR), bf16),
            pltpu.VMEM((heads, tokens, PAIR), bf16),
            pltpu.VMEM((all_blocks, BLOCK, PAIR), bf16),
            pltpu.VMEM((count, own_tokens, PAIR), bf16),
            pltpu.VMEM((count, own_tokens, PAIR), bf16),
            pltpu.VMEM((count, own_tokens, PAIR), bf16),
            pltpu.VMEM((count, tokens, PAIR), bf16),
            pltpu.VMEM((count, tokens, PAIR), bf16),
            pltpu.VMEM((count * tokens, PAIR), f32),
            pltpu.VMEM((entries + 1, BLOCK, PAIR), f32),
            pltpu.VMEM((1 << GLOBALS, BLOCK, PAIR), f32),
            whole,
            cut,
            cut,
            whole,
            pltpu.VMEM(index, i32),
            pltpu.VMEM(index, i32),
            pltpu.VMEM((2 * ROUNDS + 2, all_blocks), i32),
            pltpu.SMEM((GLOBALS,), i32),
            pltpu.SMEM(index, i32),
            pltpu.SMEM(index, i32),
            pltpu.SMEM((2 * ROUNDS + 2, all_blocks), i32),
            pltpu.SemaphoreType.DMA((16,)),
            pltpu.SemaphoreType.REGULAR,
        ]
        + [dma] * 8,
        compiler_params=pltpu.CompilerParams(
            collective_id=0, has_side_effects=True, vmem_limit_bytes=44 * 1024 * 1024
        ),
        name="attend",
    )(*operands)
    return pl.pallas_call(
        store_kernel,
        out_shape=(flat,) * 4,
        in_specs=[VMEM] * 4,
        out_specs=(HBM,) * 4,
        scratch_shapes=[pltpu.SemaphoreType.DMA((4,))],
        compiler_params=pltpu.CompilerParams(vmem_limit_bytes=1024 * 1024),
        name="store",
    )(*results)


def solution(mesh):
    rows = P(("groups", "ctx"), None)
    return jax.shard_map(
        per_device,
        mesh=mesh,
        in_specs=(rows, rows, rows, rows, P("groups"), P("groups", None), P("groups", None)),
        out_specs=(rows,) * 4,
        check_vma=False,
    )
```

```python
import functools

import jax
import jax.numpy as jnp
from jax import lax
from jax.experimental import pallas as pl
from jax.experimental.pallas import tpu as pltpu
from jax.sharding import PartitionSpec as P

HEAD_DIM = 64
GROUP_HEADS = 8
BLOCK = 64
GLOBALS = 2
ROUNDS = 3
PAIR = 2 * HEAD_DIM
NEG_FILL = -1e30
SCALE = HEAD_DIM ** (-0.5)
MESH = pl.DeviceIdType.MESH


def lanes_joined(left, right):
    return jnp.concatenate([left, right], axis=1)


def fused_kernel(
    count,
    shares,
    glob_hbm,
    owner_hbm,
    local_hbm,
    q_hbm,
    k_hbm,
    v_hbm,
    d_hbm,
    att_ref,
    gq_ref,
    gk_ref,
    gv_ref,
    kv_pack,
    qd_pack,
    kv_all,
    qd_all,
    qo_put,
    qo_got,
    gkv_put,
    gkv_got,
    acc_ref,
    chain_ref,
    glob_ref,
    q_ref,
    k_ref,
    v_ref,
    k_first,
    v_first,
    d_ref,
    owner_vec,
    local_vec,
    table_vec,
    glob_ids,
    owner_ref,
    local_ref,
    table,
    fetch,
    ready,
    kv_out,
    kv_in,
    qd_out,
    qd_in,
    qo_out,
    qo_in,
    gkv_out,
    gkv_in,
):
    me = lax.axis_index("ctx")
    heads, tokens = kv_pack.shape[:2]
    blocks = tokens // BLOCK
    own_tokens = tokens // shares
    own_blocks = own_tokens // BLOCK
    all_blocks = count * blocks
    entries = count * own_blocks * ROUNDS
    my_share = lax.rem(me, shares)
    my_head = me // shares
    my_group = my_head // GROUP_HEADS
    my_rows = pl.ds(pl.multiple_of(my_share * own_tokens, own_tokens), own_tokens)

    def differ(one, other):
        total, bit = 0, 1
        while bit < count:
            total = total + bit * lax.rem(lax.div(one, bit) + lax.div(other, bit), 2)
            bit *= 2
        return total

    half = count // 2

    def peer_of(step):
        step = jnp.int32(step)
        return differ(me, step // 2 + half * lax.rem(step, 2))

    def step_to(peer):
        gap = differ(me, peer)
        return jnp.where(gap >= half, 2 * (gap - half) + 1, 2 * gap)

    quarter = count // 4
    my_quarter = me // quarter
    inner = lax.rem(my_quarter + my_quarter // 2, 2)
    same = [*range(3 * quarter, count), *range(1, quarter)]
    unlike = [*range(quarter, 3 * quarter)]
    far = [*range(3 * quarter, count)]
    mixed = [half * (step % 2) + step // 2 for step in range(1, count)]
    width = k_ref.shape[2]

    pulls = []

    def pull(source, target):
        copy = pltpu.make_async_copy(source, target, fetch.at[len(pulls)])
        copy.start()
        pulls.append(copy)

    team = 2 * shares
    pairs = [differ(me, jnp.int32(gap)) // team for gap in range(3 * quarter, count, team)]
    for index, pair in enumerate(pairs):
        cols = pl.ds(pl.multiple_of(pair * PAIR, PAIR), PAIR)
        pull(k_hbm.at[:, cols], k_first.at[index])
        pull(v_hbm.at[:, cols], v_first.at[index])
    early = len(pulls)
    pieces = [differ(my_quarter, jnp.int32(gap)) for gap in (2, 0, 1)]
    for piece in pieces:
        cols = pl.ds(pl.multiple_of(piece * width, width), width)
        pull(k_hbm.at[:, cols], k_ref.at[piece])
        pull(v_hbm.at[:, cols], v_ref.at[piece])
    barrier = pltpu.get_barrier_semaphore()

    def greet(semaphore, gap):
        pl.semaphore_signal(
            semaphore, inc=1, device_id={"ctx": differ(me, jnp.int32(gap))}, device_id_type=MESH
        )

    for gap in same:
        greet(barrier, gap)

    @pl.when(inner == 1)
    def _():
        for gap in unlike:
            greet(barrier, gap)

    pull(q_hbm, q_ref)
    pull(d_hbm, d_ref)
    pull(owner_hbm, owner_ref)
    pull(local_hbm, local_ref)
    pull(owner_hbm, owner_vec)
    pull(local_hbm, local_vec)
    pull(glob_hbm, glob_ids)

    def pack(left, right, out_ref, head):
        out_ref[head] = lanes_joined(left[:, :HEAD_DIM], right[:, :HEAD_DIM])
        out_ref[head + 1] = lanes_joined(left[:, HEAD_DIM:], right[:, HEAD_DIM:])

    def pack_kv(index):
        pulls[early + 2 * index].wait()
        pulls[early + 2 * index + 1].wait()
        piece = pieces[index]
        for pair in range(heads // 8):
            cols = slice(pair * PAIR, (pair + 1) * PAIR)
            head = piece * (heads // 4) + 2 * pair
            pack(k_ref[piece, :, cols], v_ref[piece, :, cols], kv_pack, head)

    def pack_first(index):
        pulls[2 * index].wait()
        pulls[2 * index + 1].wait()
        pack(k_first[index], v_first[index], kv_pack, 2 * pairs[index])

    pack_first(0)

    @pl.when(inner == 0)
    def _():
        for index in range(1, len(pairs)):
            pack_first(index)
        for index in range(3):
            pack_kv(index)

    pl.semaphore_wait(barrier, 2 * quarter - 1 + (1 - inner) * 2 * quarter)

    def kv_copy(dest, came):
        return pltpu.make_async_remote_copy(
            src_ref=kv_pack.at[dest // shares].reshape(blocks, BLOCK, PAIR),
            dst_ref=kv_all.at[pl.ds(came * blocks, blocks)],
            send_sem=kv_out.at[dest],
            recv_sem=kv_in.at[came],
            device_id={"ctx": dest},
            device_id_type=MESH,
        )

    def qd_copy(dest, came):
        start = pl.multiple_of(lax.rem(dest, shares) * own_tokens, own_tokens)
        return pltpu.make_async_remote_copy(
            src_ref=qd_pack.at[dest // shares, pl.ds(start, own_tokens)],
            dst_ref=qd_all.at[came],
            send_sem=qd_out.at[dest],
            recv_sem=qd_in.at[came],
            device_id={"ctx": dest},
            device_id_type=MESH,
        )

    def row_copy(put_ref, got_ref, out_sem, in_sem):
        def copy(dest, came):
            return pltpu.make_async_remote_copy(
                src_ref=put_ref.at[dest],
                dst_ref=got_ref.at[came],
                send_sem=out_sem.at[dest],
                recv_sem=in_sem.at[came],
                device_id={"ctx": dest},
                device_id_type=MESH,
            )

        return copy

    qo_copy = row_copy(qo_put, qo_got, qo_out, qo_in)
    gkv_copy = row_copy(gkv_put, gkv_got, gkv_out, gkv_in)

    def feed(gaps):
        for gap in gaps:
            kv_copy(differ(me, jnp.int32(gap)), me).start()

    @pl.when(inner == 0)
    def _():
        for gap in unlike:
            greet(ready, gap)
        feed(mixed)

    @pl.when(inner == 1)
    def _():
        feed(far[:team])
        for index in range(1, len(pairs)):
            pack_first(index)
            feed(far[index * team : (index + 1) * team])
        for index in range(3):
            pack_kv(index)
        pl.semaphore_wait(ready, 2 * quarter)
        feed([gap for gap in mixed if gap not in far])

    local = early + 6
    pulls[local].wait()
    pulls[local + 1].wait()
    for pair in range(heads // 2):
        cols = slice(pair * PAIR, (pair + 1) * PAIR)
        pack(q_ref[:, cols], d_ref[:, cols], qd_pack, 2 * pair)
    for step in range(1, count):
        qd_copy(peer_of(step), me).start()

    for part in range(blocks):
        kv_all[me * blocks + part] = kv_pack[my_head, part * BLOCK : (part + 1) * BLOCK]
    qd_all[me] = qd_pack[my_head, my_rows, :]
    acc_ref[...] = jnp.zeros_like(acc_ref)
    glob_ref[...] = jnp.zeros_like(glob_ref)
    chain_ref[entries] = jnp.zeros_like(chain_ref[entries])

    for copy in pulls[local + 2 :]:
        copy.wait()
    first_row = my_group * ROUNDS
    rows = pl.ds(first_row, ROUNDS)
    places = owner_vec[rows, :] * blocks + local_vec[rows, :]
    block_of = lax.broadcasted_iota(jnp.int32, (ROUNDS, all_blocks), 1)
    round_of = lax.broadcasted_iota(jnp.int32, (ROUNDS, all_blocks), 0)
    turn = step_to(lax.div(block_of, blocks))
    part_of = lax.rem(block_of, blocks) - my_share * own_blocks
    order = (turn * own_blocks + part_of) * ROUNDS + round_of
    order = jnp.where((part_of >= 0) & (part_of < own_blocks), order, -1)
    lane_block = lax.broadcasted_iota(jnp.int32, (1, all_blocks), 1)

    def link(step, carry):
        before, last = carry
        peer = peer_of(step)
        for part in range(own_blocks):
            block = peer * blocks + my_share * own_blocks + part
            for kind in range(ROUNDS):
                entry = (step * own_blocks + part) * ROUNDS + kind
                place = (
                    owner_ref[first_row + kind, block] * blocks + local_ref[first_row + kind, block]
                )
                before = jnp.where((places == place) & (order > entry), entry, before)
                last = jnp.where(lane_block == place, entry, last)
        return before, last

    before, last = lax.fori_loop(
        0,
        count,
        link,
        (
            jnp.full((ROUNDS, all_blocks), entries, jnp.int32),
            jnp.full((1, all_blocks), entries, jnp.int32),
        ),
    )
    which = jnp.zeros((1, all_blocks), jnp.int32)
    for index in range(GLOBALS):
        which += jnp.where(lane_block == glob_ids[index], 1 << index, 0)
    table_vec[0:ROUNDS, :] = places
    table_vec[ROUNDS : 2 * ROUNDS, :] = before
    table_vec[2 * ROUNDS : 2 * ROUNDS + 1, :] = last
    table_vec[2 * ROUNDS + 1 : 2 * ROUNDS + 2, :] = which
    to_scalar = pltpu.make_async_copy(table_vec, table, fetch.at[len(pulls)])
    to_scalar.start()
    to_scalar.wait()

    for step in range(1, count):
        peer = peer_of(step)
        kv_copy(peer, peer).wait_recv()

    lane = lax.broadcasted_iota(jnp.int32, (BLOCK, PAIR), 1)
    low = lane < HEAD_DIM
    row_lane = lax.broadcasted_iota(jnp.int32, (1, PAIR), 1)
    contract_last = (((1,), (1,)), ((), ()))
    contract_first = (((0,), (0,)), ((), ()))

    def load(peer, part):
        block = peer * blocks + my_share * own_blocks + part
        qd = qd_all[peer, part * BLOCK : (part + 1) * BLOCK, :]
        near = [lax.rem(block + all_blocks - 1, all_blocks), lax.rem(block + 1, all_blocks), block]
        spots = near + [glob_ids[kind] for kind in range(GLOBALS)]
        spots = spots + [table[kind, block] for kind in range(ROUNDS)]
        kv = jnp.concatenate([kv_all[p] for p in spots], axis=0)
        zero = jnp.zeros_like(qd)
        diag = jnp.concatenate(
            [jnp.where(low, qd * jnp.bfloat16(SCALE), zero), jnp.where(low, zero, qd)], axis=0
        )
        both = lax.dot_general(diag, kv, contract_last, preferred_element_type=jnp.float32)
        return block, near, qd, kv, diag, both

    def soften(block, both):
        scores = both[:BLOCK]
        bias = jnp.where(
            row_lane < BLOCK,
            jnp.where(block == 0, NEG_FILL, 0.0),
            jnp.where(block == all_blocks - 1, NEG_FILL, 0.0),
        ).astype(jnp.float32)
        scores = lanes_joined(scores[:, :PAIR] + bias, scores[:, PAIR:])
        row_max = jnp.max(scores, axis=1, keepdims=True)
        weights = jnp.exp(scores - row_max)
        probs = weights * (1.0 / jnp.sum(weights, axis=1, keepdims=True))
        return probs, probs.astype(jnp.bfloat16)

    def finish(peer, step, part, block, qd, kv, diag, both, probs, probs_b, attended):
        row_dot = jnp.sum(
            jnp.where(low, 0.0, qd.astype(jnp.float32) * attended.astype(jnp.float32)),
            axis=1,
            keepdims=True,
        )
        dscore = (probs * (both[BLOCK:] - row_dot)).astype(jnp.bfloat16)
        grad_q = jnp.dot(dscore, kv, preferred_element_type=jnp.float32) * SCALE
        qo_put[peer, part * BLOCK : (part + 1) * BLOCK, :] = jnp.where(
            low, grad_q.astype(jnp.bfloat16), attended
        )
        terms = lax.dot_general(
            jnp.concatenate([dscore, probs_b], axis=0),
            diag,
            contract_first,
            preferred_element_type=jnp.float32,
        )
        return terms

    def front(peer, step):
        stage = [load(peer, part) for part in range(own_blocks)]
        soft = [soften(block, both) for block, _, _, _, _, both in stage]
        seen = [
            jnp.dot(probs_b, kept[3], preferred_element_type=jnp.float32).astype(jnp.bfloat16)
            for kept, (_, probs_b) in zip(stage, soft)
        ]
        return [
            (
                block,
                near,
                finish(peer, step, part, block, qd, kv, diag, both, *soft[part], seen[part]),
            )
            for part, (block, near, qd, kv, diag, both) in enumerate(stage)
        ]

    def step_of(step, carry):
        peer = peer_of(step)

        @pl.when(step > 0)
        def _():
            qd_copy(peer, peer).wait_recv()

        done = front(peer, step)
        for part, (block, near, terms) in enumerate(done):
            for kind in range(3):
                spot = pl.ds(pl.multiple_of(near[kind] * BLOCK, BLOCK), BLOCK)
                acc_ref[spot, :] += terms[kind * BLOCK : (kind + 1) * BLOCK]
            for kind in range(ROUNDS):
                start = (3 + GLOBALS + kind) * BLOCK
                term = terms[start : start + BLOCK].astype(jnp.bfloat16).astype(jnp.float32)
                entry = (step * own_blocks + part) * ROUNDS + kind
                chain_ref[entry] = chain_ref[table[ROUNDS + kind, block]] + term
        shared = functools.reduce(
            jnp.add, [terms[3 * BLOCK : (3 + GLOBALS) * BLOCK] for _, _, terms in done]
        )
        for index in range(GLOBALS):
            own = shared[index * BLOCK : (index + 1) * BLOCK]
            for mix in range(1, 1 << GLOBALS):
                if mix >> index & 1:
                    glob_ref[mix] += own

        @pl.when(step > 1)
        def _():
            qo_copy(peer_of(step - 1), me).start()

        return carry

    lax.fori_loop(0, count, step_of, 0)
    qo_copy(peer_of(count - 1), me).start()

    def total_of(step, carry):
        dest = peer_of(step)
        for part in range(blocks):
            block = dest * blocks + part
            spot = pl.ds(pl.multiple_of(block * BLOCK, BLOCK), BLOCK)
            total = acc_ref[spot, :] + chain_ref[table[2 * ROUNDS, block]]
            total = total + glob_ref[table[2 * ROUNDS + 1, block]]
            gkv_put[dest, part * BLOCK : (part + 1) * BLOCK, :] = total.astype(jnp.bfloat16)

        @pl.when(step > 0)
        def _():
            gkv_copy(dest, me).start()

        return carry

    lax.fori_loop(0, count, total_of, 0)
    qo_got[me] = qo_put[me]
    gkv_got[me] = gkv_put[me]

    for step in range(1, count):
        peer = peer_of(step)
        qo_copy(peer, peer).wait_recv()
    for pair in range(heads // 2):
        cols = slice(pair * PAIR, (pair + 1) * PAIR)
        for share in range(shares):
            part = slice(share * own_tokens, (share + 1) * own_tokens)
            even = qo_got[2 * pair * shares + share]
            odd = qo_got[(2 * pair + 1) * shares + share]
            gq_ref[part, cols] = lanes_joined(even[:, :HEAD_DIM], odd[:, :HEAD_DIM])
            att_ref[part, cols] = lanes_joined(even[:, HEAD_DIM:], odd[:, HEAD_DIM:])
    for step in range(1, count):
        peer = peer_of(step)
        kv_copy(peer, me).wait_send()
        qd_copy(peer, me).wait_send()
        qo_copy(peer, me).wait_send()

    def head_of(head):
        for share in range(shares):
            source = head * shares + share

            @pl.when(source != me)
            def _():
                gkv_copy(source, source).wait_recv()

        total = gkv_got[head * shares]
        if shares > 1:
            total = total.astype(jnp.float32)
            for share in range(1, shares):
                total += gkv_got[head * shares + share].astype(jnp.float32)
            total = total.astype(jnp.bfloat16)
        return total

    for gap in range(heads // 2):
        if gap == heads // 2 - 1:
            for step in range(1, count):
                gkv_copy(peer_of(step), me).wait_send()
        pair = differ(my_head // 2, jnp.int32(gap))
        cols = pl.ds(pl.multiple_of(pair * PAIR, PAIR), PAIR)
        even = head_of(2 * pair)
        odd = head_of(2 * pair + 1)
        gk_ref[:, cols] = lanes_joined(even[:, :HEAD_DIM], odd[:, :HEAD_DIM])
        gv_ref[:, cols] = lanes_joined(even[:, HEAD_DIM:], odd[:, HEAD_DIM:])


def store_kernel(*refs):
    size = (len(refs) - 1) // 2
    pushes = [
        pltpu.make_async_copy(refs[index], refs[size + index], refs[-1].at[index])
        for index in range(size)
    ]
    for push in pushes:
        push.start()
    for push in pushes:
        push.wait()


VMEM = pl.BlockSpec(memory_space=pltpu.VMEM)
HBM = pl.BlockSpec(memory_space=pltpu.HBM)


def per_device(query, key, value, cotangent, global_ids, rand_owner, rand_local):
    tokens, features = query.shape
    blocks = tokens // BLOCK
    heads = features // HEAD_DIM
    count = lax.axis_size("ctx")
    shares = count // heads
    own_blocks = blocks // shares
    own_tokens = own_blocks * BLOCK
    all_blocks = count * blocks
    entries = count * own_blocks * ROUNDS
    shape = jax.ShapeDtypeStruct
    bf16, f32, i32 = jnp.bfloat16, jnp.float32, jnp.int32

    operands = [
        pltpu.with_memory_space_constraint(operand, pltpu.HBM)
        for operand in (global_ids, rand_owner.T, rand_local.T, query, key, value, cotangent)
    ]
    dma = pltpu.SemaphoreType.DMA((count,))
    flat = shape((tokens, features), bf16)
    whole = pltpu.VMEM((tokens, features), bf16)
    cut = pltpu.VMEM((4, tokens, features // 4), bf16)
    first = pltpu.VMEM((heads // 8, tokens, PAIR), bf16)
    index = (rand_owner.shape[1], all_blocks)
    results = pl.pallas_call(
        functools.partial(fused_kernel, count, shares),
        out_shape=(flat,) * 4,
        in_specs=[HBM] * 7,
        out_specs=(VMEM,) * 4,
        scratch_shapes=[
            pltpu.VMEM((heads, tokens, PAIR), bf16),
            pltpu.VMEM((heads, tokens, PAIR), bf16),
            pltpu.VMEM((all_blocks, BLOCK, PAIR), bf16),
            pltpu.VMEM((count, own_tokens, PAIR), bf16),
            pltpu.VMEM((count, own_tokens, PAIR), bf16),
            pltpu.VMEM((count, own_tokens, PAIR), bf16),
            pltpu.VMEM((count, tokens, PAIR), bf16),
            pltpu.VMEM((count, tokens, PAIR), bf16),
            pltpu.VMEM((count * tokens, PAIR), f32),
            pltpu.VMEM((entries + 1, BLOCK, PAIR), f32),
            pltpu.VMEM((1 << GLOBALS, BLOCK, PAIR), f32),
            whole,
            cut,
            cut,
            first,
            first,
            whole,
            pltpu.VMEM(index, i32),
            pltpu.VMEM(index, i32),
            pltpu.VMEM((2 * ROUNDS + 2, all_blocks), i32),
            pltpu.SMEM((GLOBALS,), i32),
            pltpu.SMEM(index, i32),
            pltpu.SMEM(index, i32),
            pltpu.SMEM((2 * ROUNDS + 2, all_blocks), i32),
            pltpu.SemaphoreType.DMA((2 * (heads // 8) + 14,)),
            pltpu.SemaphoreType.REGULAR,
        ]
        + [dma] * 8,
        compiler_params=pltpu.CompilerParams(
            collective_id=0, has_side_effects=True, vmem_limit_bytes=44 * 1024 * 1024
        ),
        name="attend",
    )(*operands)
    return pl.pallas_call(
        store_kernel,
        out_shape=(flat,) * 4,
        in_specs=[VMEM] * 4,
        out_specs=(HBM,) * 4,
        scratch_shapes=[pltpu.SemaphoreType.DMA((4,))],
        compiler_params=pltpu.CompilerParams(vmem_limit_bytes=1024 * 1024),
        name="store",
    )(*results)


def solution(mesh):
    rows = P(("groups", "ctx"), None)
    return jax.shard_map(
        per_device,
        mesh=mesh,
        in_specs=(rows, rows, rows, rows, P("groups"), P("groups", None), P("groups", None)),
        out_specs=(rows,) * 4,
        check_vma=False,
    )
```

```python
import functools

import jax
import jax.numpy as jnp
from jax import lax
from jax.experimental import pallas as pl
from jax.experimental.pallas import tpu as pltpu
from jax.sharding import PartitionSpec as P

HEAD_DIM = 64
GROUP_HEADS = 8
BLOCK = 64
GLOBALS = 2
ROUNDS = 3
PAIR = 2 * HEAD_DIM
NEG_FILL = -1e30
SCALE = HEAD_DIM ** (-0.5)
MESH = pl.DeviceIdType.MESH


def lanes_joined(left, right):
    return jnp.concatenate([left, right], axis=1)


def fused_kernel(
    count,
    shares,
    glob_hbm,
    owner_hbm,
    local_hbm,
    q_hbm,
    k_hbm,
    v_hbm,
    d_hbm,
    att_ref,
    gq_ref,
    gk_ref,
    gv_ref,
    kv_pack,
    qd_pack,
    kv_all,
    qd_all,
    qo_put,
    qo_got,
    gkv_put,
    gkv_got,
    acc_ref,
    chain_ref,
    glob_ref,
    q_ref,
    k_ref,
    v_ref,
    k_first,
    v_first,
    d_ref,
    owner_vec,
    local_vec,
    table_vec,
    glob_ids,
    owner_ref,
    local_ref,
    table,
    fetch,
    ready,
    kv_out,
    kv_in,
    qd_out,
    qd_in,
    qo_out,
    qo_in,
    gkv_out,
    gkv_in,
):
    me = lax.axis_index("ctx")
    heads, tokens = kv_pack.shape[:2]
    blocks = tokens // BLOCK
    own_tokens = tokens // shares
    own_blocks = own_tokens // BLOCK
    all_blocks = count * blocks
    entries = count * own_blocks * ROUNDS
    my_share = lax.rem(me, shares)
    my_head = me // shares
    my_group = my_head // GROUP_HEADS
    my_rows = pl.ds(pl.multiple_of(my_share * own_tokens, own_tokens), own_tokens)

    def differ(one, other):
        total, bit = 0, 1
        while bit < count:
            total = total + bit * lax.rem(lax.div(one, bit) + lax.div(other, bit), 2)
            bit *= 2
        return total

    half = count // 2

    def peer_of(step):
        step = jnp.int32(step)
        return differ(me, step // 2 + half * lax.rem(step, 2))

    def step_to(peer):
        gap = differ(me, peer)
        return jnp.where(gap >= half, 2 * (gap - half) + 1, 2 * gap)

    quarter = count // 4
    my_quarter = me // quarter
    inner = lax.rem(my_quarter + my_quarter // 2, 2)
    same = [*range(3 * quarter, count), *range(1, quarter)]
    unlike = [*range(quarter, 3 * quarter)]
    far = [*range(3 * quarter, count)]
    mixed = [half * (step % 2) + step // 2 for step in range(1, count)]
    width = k_ref.shape[2]

    pulls = []

    def pull(source, target):
        copy = pltpu.make_async_copy(source, target, fetch.at[len(pulls)])
        copy.start()
        pulls.append(copy)

    team = 2 * shares
    pairs = [differ(me, jnp.int32(gap)) // team for gap in range(3 * quarter, count, team)]
    for index, pair in enumerate(pairs):
        cols = pl.ds(pl.multiple_of(pair * PAIR, PAIR), PAIR)
        pull(k_hbm.at[:, cols], k_first.at[index])
        pull(v_hbm.at[:, cols], v_first.at[index])
    early = len(pulls)
    pieces = [differ(my_quarter, jnp.int32(gap)) for gap in (2, 0, 1)]
    for piece in pieces:
        cols = pl.ds(pl.multiple_of(piece * width, width), width)
        pull(k_hbm.at[:, cols], k_ref.at[piece])
        pull(v_hbm.at[:, cols], v_ref.at[piece])
    barrier = pltpu.get_barrier_semaphore()

    def greet(semaphore, gap):
        pl.semaphore_signal(
            semaphore, inc=1, device_id={"ctx": differ(me, jnp.int32(gap))}, device_id_type=MESH
        )

    for gap in same:
        greet(barrier, gap)

    @pl.when(inner == 1)
    def _():
        for gap in unlike:
            greet(barrier, gap)

    pull(q_hbm, q_ref)
    pull(d_hbm, d_ref)
    pull(owner_hbm, owner_ref)
    pull(local_hbm, local_ref)
    pull(owner_hbm, owner_vec)
    pull(local_hbm, local_vec)
    pull(glob_hbm, glob_ids)

    def pack(left, right, out_ref, head):
        out_ref[head] = lanes_joined(left[:, :HEAD_DIM], right[:, :HEAD_DIM])
        out_ref[head + 1] = lanes_joined(left[:, HEAD_DIM:], right[:, HEAD_DIM:])

    def pack_kv(index):
        pulls[early + 2 * index].wait()
        pulls[early + 2 * index + 1].wait()
        piece = pieces[index]
        for pair in range(heads // 8):
            cols = slice(pair * PAIR, (pair + 1) * PAIR)
            head = piece * (heads // 4) + 2 * pair
            pack(k_ref[piece, :, cols], v_ref[piece, :, cols], kv_pack, head)

    def pack_first(index):
        pulls[2 * index].wait()
        pulls[2 * index + 1].wait()
        pack(k_first[index], v_first[index], kv_pack, 2 * pairs[index])

    pack_first(0)

    @pl.when(inner == 0)
    def _():
        for index in range(1, len(pairs)):
            pack_first(index)
        for index in range(3):
            pack_kv(index)

    pl.semaphore_wait(barrier, 2 * quarter - 1 + (1 - inner) * 2 * quarter)

    def kv_copy(dest, came):
        return pltpu.make_async_remote_copy(
            src_ref=kv_pack.at[dest // shares].reshape(blocks, BLOCK, PAIR),
            dst_ref=kv_all.at[pl.ds(came * blocks, blocks)],
            send_sem=kv_out.at[dest],
            recv_sem=kv_in.at[came],
            device_id={"ctx": dest},
            device_id_type=MESH,
        )

    def qd_copy(dest, came):
        start = pl.multiple_of(lax.rem(dest, shares) * own_tokens, own_tokens)
        return pltpu.make_async_remote_copy(
            src_ref=qd_pack.at[dest // shares, pl.ds(start, own_tokens)],
            dst_ref=qd_all.at[came],
            send_sem=qd_out.at[dest],
            recv_sem=qd_in.at[came],
            device_id={"ctx": dest},
            device_id_type=MESH,
        )

    def row_copy(put_ref, got_ref, out_sem, in_sem):
        def copy(dest, came):
            return pltpu.make_async_remote_copy(
                src_ref=put_ref.at[dest],
                dst_ref=got_ref.at[came],
                send_sem=out_sem.at[dest],
                recv_sem=in_sem.at[came],
                device_id={"ctx": dest},
                device_id_type=MESH,
            )

        return copy

    qo_copy = row_copy(qo_put, qo_got, qo_out, qo_in)
    gkv_copy = row_copy(gkv_put, gkv_got, gkv_out, gkv_in)

    def feed(gaps):
        for gap in gaps:
            kv_copy(differ(me, jnp.int32(gap)), me).start()

    @pl.when(inner == 0)
    def _():
        for gap in unlike:
            greet(ready, gap)
        feed(mixed)

    @pl.when(inner == 1)
    def _():
        feed(far[:team])
        for index in range(1, len(pairs)):
            pack_first(index)
            feed(far[index * team : (index + 1) * team])
        for index in range(3):
            pack_kv(index)
        pl.semaphore_wait(ready, 2 * quarter)
        feed([gap for gap in mixed if gap not in far])

    local = early + 6
    pulls[local].wait()
    pulls[local + 1].wait()
    for pair in range(heads // 2):
        cols = slice(pair * PAIR, (pair + 1) * PAIR)
        pack(q_ref[:, cols], d_ref[:, cols], qd_pack, 2 * pair)
    for step in range(1, count):
        qd_copy(peer_of(step), me).start()

    for part in range(blocks):
        kv_all[me * blocks + part] = kv_pack[my_head, part * BLOCK : (part + 1) * BLOCK]
    qd_all[me] = qd_pack[my_head, my_rows, :]
    acc_ref[...] = jnp.zeros_like(acc_ref)
    glob_ref[...] = jnp.zeros_like(glob_ref)
    chain_ref[entries] = jnp.zeros_like(chain_ref[entries])

    for copy in pulls[local + 2 :]:
        copy.wait()
    first_row = my_group * ROUNDS
    rows = pl.ds(first_row, ROUNDS)
    places = owner_vec[rows, :] * blocks + local_vec[rows, :]
    block_of = lax.broadcasted_iota(jnp.int32, (ROUNDS, all_blocks), 1)
    round_of = lax.broadcasted_iota(jnp.int32, (ROUNDS, all_blocks), 0)
    turn = step_to(lax.div(block_of, blocks))
    part_of = lax.rem(block_of, blocks) - my_share * own_blocks
    order = (turn * own_blocks + part_of) * ROUNDS + round_of
    order = jnp.where((part_of >= 0) & (part_of < own_blocks), order, -1)
    lane_block = lax.broadcasted_iota(jnp.int32, (1, all_blocks), 1)

    def link(step, carry):
        before, last = carry
        peer = peer_of(step)
        for part in range(own_blocks):
            block = peer * blocks + my_share * own_blocks + part
            for kind in range(ROUNDS):
                entry = (step * own_blocks + part) * ROUNDS + kind
                place = (
                    owner_ref[first_row + kind, block] * blocks + local_ref[first_row + kind, block]
                )
                before = jnp.where((places == place) & (order > entry), entry, before)
                last = jnp.where(lane_block == place, entry, last)
        return before, last

    before, last = lax.fori_loop(
        0,
        count,
        link,
        (
            jnp.full((ROUNDS, all_blocks), entries, jnp.int32),
            jnp.full((1, all_blocks), entries, jnp.int32),
        ),
    )
    which = jnp.zeros((1, all_blocks), jnp.int32)
    for index in range(GLOBALS):
        which += jnp.where(lane_block == glob_ids[index], 1 << index, 0)
    table_vec[0:ROUNDS, :] = places
    table_vec[ROUNDS : 2 * ROUNDS, :] = before
    table_vec[2 * ROUNDS : 2 * ROUNDS + 1, :] = last
    table_vec[2 * ROUNDS + 1 : 2 * ROUNDS + 2, :] = which
    to_scalar = pltpu.make_async_copy(table_vec, table, fetch.at[len(pulls)])
    to_scalar.start()
    to_scalar.wait()

    for step in range(1, count):
        peer = peer_of(step)
        kv_copy(peer, peer).wait_recv()

    lane = lax.broadcasted_iota(jnp.int32, (BLOCK, PAIR), 1)
    low = lane < HEAD_DIM
    row_lane = lax.broadcasted_iota(jnp.int32, (1, PAIR), 1)
    contract_last = (((1,), (1,)), ((), ()))
    contract_first = (((0,), (0,)), ((), ()))

    def load(peer, part):
        block = peer * blocks + my_share * own_blocks + part
        qd = qd_all[peer, part * BLOCK : (part + 1) * BLOCK, :]
        near = [lax.rem(block + all_blocks - 1, all_blocks), lax.rem(block + 1, all_blocks), block]
        spots = near + [glob_ids[kind] for kind in range(GLOBALS)]
        spots = spots + [table[kind, block] for kind in range(ROUNDS)]
        kv = jnp.concatenate([kv_all[p] for p in spots], axis=0)
        zero = jnp.zeros_like(qd)
        diag = jnp.concatenate(
            [jnp.where(low, qd * jnp.bfloat16(SCALE), zero), jnp.where(low, zero, qd)], axis=0
        )
        both = lax.dot_general(diag, kv, contract_last, preferred_element_type=jnp.float32)
        return block, near, qd, kv, diag, both

    def soften(block, both):
        scores = both[:BLOCK]
        bias = jnp.where(
            row_lane < BLOCK,
            jnp.where(block == 0, NEG_FILL, 0.0),
            jnp.where(block == all_blocks - 1, NEG_FILL, 0.0),
        ).astype(jnp.float32)
        scores = lanes_joined(scores[:, :PAIR] + bias, scores[:, PAIR:])
        row_max = jnp.max(scores, axis=1, keepdims=True)
        weights = jnp.exp(scores - row_max)
        probs = weights * (1.0 / jnp.sum(weights, axis=1, keepdims=True))
        return probs, probs.astype(jnp.bfloat16)

    def finish(peer, step, part, block, qd, kv, diag, both, probs, probs_b, attended):
        row_dot = jnp.sum(
            jnp.where(low, 0.0, qd.astype(jnp.float32) * attended.astype(jnp.float32)),
            axis=1,
            keepdims=True,
        )
        dscore = (probs * (both[BLOCK:] - row_dot)).astype(jnp.bfloat16)
        grad_q = jnp.dot(dscore, kv, preferred_element_type=jnp.float32) * SCALE
        qo_put[peer, part * BLOCK : (part + 1) * BLOCK, :] = jnp.where(
            low, grad_q.astype(jnp.bfloat16), attended
        )
        terms = lax.dot_general(
            jnp.concatenate([dscore, probs_b], axis=0),
            diag,
            contract_first,
            preferred_element_type=jnp.float32,
        )
        return terms

    def front(peer, step):
        stage = [load(peer, part) for part in range(own_blocks)]
        soft = [soften(block, both) for block, _, _, _, _, both in stage]
        seen = [
            jnp.dot(probs_b, kept[3], preferred_element_type=jnp.float32).astype(jnp.bfloat16)
            for kept, (_, probs_b) in zip(stage, soft)
        ]
        return [
            (
                block,
                near,
                finish(peer, step, part, block, qd, kv, diag, both, *soft[part], seen[part]),
            )
            for part, (block, near, qd, kv, diag, both) in enumerate(stage)
        ]

    def step_of(step, carry):
        peer = peer_of(step)

        @pl.when(step > 0)
        def _():
            qd_copy(peer, peer).wait_recv()

        done = front(peer, step)
        for part, (block, near, terms) in enumerate(done):
            for kind in range(3):
                spot = pl.ds(pl.multiple_of(near[kind] * BLOCK, BLOCK), BLOCK)
                acc_ref[spot, :] += terms[kind * BLOCK : (kind + 1) * BLOCK]
            for kind in range(ROUNDS):
                start = (3 + GLOBALS + kind) * BLOCK
                term = terms[start : start + BLOCK].astype(jnp.bfloat16).astype(jnp.float32)
                entry = (step * own_blocks + part) * ROUNDS + kind
                chain_ref[entry] = chain_ref[table[ROUNDS + kind, block]] + term
        shared = functools.reduce(
            jnp.add, [terms[3 * BLOCK : (3 + GLOBALS) * BLOCK] for _, _, terms in done]
        )
        for index in range(GLOBALS):
            own = shared[index * BLOCK : (index + 1) * BLOCK]
            for mix in range(1, 1 << GLOBALS):
                if mix >> index & 1:
                    glob_ref[mix] += own

        @pl.when(step > 0)
        def _():
            qo_copy(peer, me).start()

        return carry

    lax.fori_loop(0, count, step_of, 0)

    def total_of(step, carry):
        dest = peer_of(step)
        for part in range(blocks):
            block = dest * blocks + part
            spot = pl.ds(pl.multiple_of(block * BLOCK, BLOCK), BLOCK)
            total = acc_ref[spot, :] + chain_ref[table[2 * ROUNDS, block]]
            total = total + glob_ref[table[2 * ROUNDS + 1, block]]
            gkv_put[dest, part * BLOCK : (part + 1) * BLOCK, :] = total.astype(jnp.bfloat16)

        @pl.when(step > 0)
        def _():
            gkv_copy(dest, me).start()

        return carry

    lax.fori_loop(0, count, total_of, 0)
    qo_got[me] = qo_put[me]
    gkv_got[me] = gkv_put[me]

    for step in range(1, count):
        peer = peer_of(step)
        qo_copy(peer, peer).wait_recv()
    for pair in range(heads // 2):
        cols = slice(pair * PAIR, (pair + 1) * PAIR)
        for share in range(shares):
            part = slice(share * own_tokens, (share + 1) * own_tokens)
            even = qo_got[2 * pair * shares + share]
            odd = qo_got[(2 * pair + 1) * shares + share]
            gq_ref[part, cols] = lanes_joined(even[:, :HEAD_DIM], odd[:, :HEAD_DIM])
            att_ref[part, cols] = lanes_joined(even[:, HEAD_DIM:], odd[:, HEAD_DIM:])
    for step in range(1, count):
        peer = peer_of(step)
        kv_copy(peer, me).wait_send()
        qd_copy(peer, me).wait_send()
        qo_copy(peer, me).wait_send()

    def head_of(head):
        for share in range(shares):
            source = head * shares + share

            @pl.when(source != me)
            def _():
                gkv_copy(source, source).wait_recv()

        total = gkv_got[head * shares]
        if shares > 1:
            total = total.astype(jnp.float32)
            for share in range(1, shares):
                total += gkv_got[head * shares + share].astype(jnp.float32)
            total = total.astype(jnp.bfloat16)
        return total

    for gap in range(heads // 2):
        if gap == heads // 2 - 1:
            for step in range(1, count):
                gkv_copy(peer_of(step), me).wait_send()
        pair = differ(my_head // 2, jnp.int32(gap))
        cols = pl.ds(pl.multiple_of(pair * PAIR, PAIR), PAIR)
        even = head_of(2 * pair)
        odd = head_of(2 * pair + 1)
        gk_ref[:, cols] = lanes_joined(even[:, :HEAD_DIM], odd[:, :HEAD_DIM])
        gv_ref[:, cols] = lanes_joined(even[:, HEAD_DIM:], odd[:, HEAD_DIM:])


def store_kernel(*refs):
    size = (len(refs) - 1) // 2
    pushes = [
        pltpu.make_async_copy(refs[index], refs[size + index], refs[-1].at[index])
        for index in range(size)
    ]
    for push in pushes:
        push.start()
    for push in pushes:
        push.wait()


VMEM = pl.BlockSpec(memory_space=pltpu.VMEM)
HBM = pl.BlockSpec(memory_space=pltpu.HBM)


def per_device(query, key, value, cotangent, global_ids, rand_owner, rand_local):
    tokens, features = query.shape
    blocks = tokens // BLOCK
    heads = features // HEAD_DIM
    count = lax.axis_size("ctx")
    shares = count // heads
    own_blocks = blocks // shares
    own_tokens = own_blocks * BLOCK
    all_blocks = count * blocks
    entries = count * own_blocks * ROUNDS
    shape = jax.ShapeDtypeStruct
    bf16, f32, i32 = jnp.bfloat16, jnp.float32, jnp.int32

    operands = [
        pltpu.with_memory_space_constraint(operand, pltpu.HBM)
        for operand in (global_ids, rand_owner.T, rand_local.T, query, key, value, cotangent)
    ]
    dma = pltpu.SemaphoreType.DMA((count,))
    flat = shape((tokens, features), bf16)
    whole = pltpu.VMEM((tokens, features), bf16)
    cut = pltpu.VMEM((4, tokens, features // 4), bf16)
    first = pltpu.VMEM((heads // 8, tokens, PAIR), bf16)
    index = (rand_owner.shape[1], all_blocks)
    results = pl.pallas_call(
        functools.partial(fused_kernel, count, shares),
        out_shape=(flat,) * 4,
        in_specs=[HBM] * 7,
        out_specs=(VMEM,) * 4,
        scratch_shapes=[
            pltpu.VMEM((heads, tokens, PAIR), bf16),
            pltpu.VMEM((heads, tokens, PAIR), bf16),
            pltpu.VMEM((all_blocks, BLOCK, PAIR), bf16),
            pltpu.VMEM((count, own_tokens, PAIR), bf16),
            pltpu.VMEM((count, own_tokens, PAIR), bf16),
            pltpu.VMEM((count, own_tokens, PAIR), bf16),
            pltpu.VMEM((count, tokens, PAIR), bf16),
            pltpu.VMEM((count, tokens, PAIR), bf16),
            pltpu.VMEM((count * tokens, PAIR), f32),
            pltpu.VMEM((entries + 1, BLOCK, PAIR), f32),
            pltpu.VMEM((1 << GLOBALS, BLOCK, PAIR), f32),
            whole,
            cut,
            cut,
            first,
            first,
            whole,
            pltpu.VMEM(index, i32),
            pltpu.VMEM(index, i32),
            pltpu.VMEM((2 * ROUNDS + 2, all_blocks), i32),
            pltpu.SMEM((GLOBALS,), i32),
            pltpu.SMEM(index, i32),
            pltpu.SMEM(index, i32),
            pltpu.SMEM((2 * ROUNDS + 2, all_blocks), i32),
            pltpu.SemaphoreType.DMA((2 * (heads // 8) + 14,)),
            pltpu.SemaphoreType.REGULAR,
        ]
        + [dma] * 8,
        compiler_params=pltpu.CompilerParams(
            collective_id=0, has_side_effects=True, vmem_limit_bytes=44 * 1024 * 1024
        ),
        name="attend",
    )(*operands)
    return pl.pallas_call(
        store_kernel,
        out_shape=(flat,) * 4,
        in_specs=[VMEM] * 4,
        out_specs=(HBM,) * 4,
        scratch_shapes=[pltpu.SemaphoreType.DMA((4,))],
        compiler_params=pltpu.CompilerParams(vmem_limit_bytes=1024 * 1024),
        name="store",
    )(*results)


def solution(mesh):
    rows = P(("groups", "ctx"), None)
    return jax.shard_map(
        per_device,
        mesh=mesh,
        in_specs=(rows, rows, rows, rows, P("groups"), P("groups", None), P("groups", None)),
        out_specs=(rows,) * 4,
        check_vma=False,
    )
```
